256 devices in a mesh: tm: 8 (over y, core), vert: 32 (over z, x).
Axes of the slice: x: 4, y: 4, z: 8, core: 2. Of those that a mesh axis runs over, the one named last changes fastest.
Arguments:
- features: bfloat16 [32, 16384, 128], P('tm', 'vert'), may hold values from -6 to 6
- tile_cols: int32 [32, 128, 8], P('tm', 'vert'), may hold values from 0 to 127, as said below
- tile_vals: bfloat16 [32, 128, 8, 128, 128], P('tm', 'vert'), may hold values from -0.1875 to 0.1875
- space_weight: bfloat16 [128, 128], replicated, may hold values from -0.5 to 0.5
- positions: bfloat16 [32, 128], replicated, may hold values from -6 to 6
- attn_proj: bfloat16 [128, 384], replicated, may hold values from -0.5 to 0.5
- attn_out: bfloat16 [128, 128], replicated, may hold values from -0.5 to 0.5
- norm_gain: float32 [128], replicated, may hold values from 0.1 to 1.9
- mlp_up: bfloat16 [128, 512], replicated, may hold values from -0.5 to 0.5
- mlp_down: bfloat16 [512, 128], replicated, may hold values from -0.25 to 0.25
Outputs:
- embedded: bfloat16 [32, 16384, 128], P('tm', 'vert')
The draws below stay inside these ranges and needn't reach their ends.
Inputs may be any that keep to these rules, and one draw needn't show every extreme that they name: `tile_cols`: for each snapshot and each group of 4 consecutive row blocks, the listed column blocks name at most two distinct blocks among those of any one group (blocks c with the same c // 4), and exactly two for some group.
All inputs are finite; a program needn't handle non-finite values.
Results may differ from the reference program's by a relative error of at most 0.0064.
Values may be sent and summed in bfloat16 or wider, within the bound.
A program may use at most 128 MiB of HBM per device.

```python
import math
import jax
import jax.numpy as jnp
from jax import lax

D = 128
HEADS = 16
FFN = 512
TB = 128
TILES = 8
SNAPS = 32
BLK_DEV = 4
NBLK = 128
VERTS = 16384
VT = 64
N_VERT = 32


def draw_tile_cols(key, part):
    key_first, key_second, key_owner, key_slot = jax.random.split(jax.random.fold_in(key, 11), 4)
    first = jax.random.randint(key_first, (SNAPS, N_VERT, N_VERT), 0, BLK_DEV, dtype=jnp.int32)
    second = (first + jax.random.randint(key_second, (SNAPS, N_VERT, N_VERT), 1, BLK_DEV, dtype=jnp.int32)) % BLK_DEV
    choices_all = jnp.stack([first, second], axis=-1).reshape(SNAPS, N_VERT, N_VERT * 2)
    owners = jax.random.randint(key_owner, (SNAPS, N_VERT, BLK_DEV * TILES), 0, N_VERT, dtype=jnp.int32)
    slots = jax.random.randint(key_slot, (SNAPS, N_VERT, BLK_DEV * TILES), 0, 2, dtype=jnp.int32)
    owners = owners.at[:, :, 0].set(0).at[:, :, 1].set(0)
    slots = slots.at[:, :, 0].set(0).at[:, :, 1].set(1)
    local_blk = jnp.take_along_axis(choices_all, owners * 2 + slots, axis=2)
    columns = owners * BLK_DEV + local_blk
    return columns.reshape(SNAPS, N_VERT * BLK_DEV, TILES).astype(jnp.int32)


def level_of(rng, dims, cuts, least, high):
    def one(position, blocks):
        draws = jax.random.uniform(jax.random.fold_in(jax.random.fold_in(rng, 6), position), (blocks,), jnp.float32, least / len(cuts), high / len(cuts))
        return jnp.repeat(jnp.exp(draws), dims[position] // blocks).reshape((-1,) + (1,) * (len(dims) - position - 1))

    factor_of = one(*cuts[0])
    for cut in cuts[1:]:
        factor_of = factor_of * one(*cut)
    return factor_of


def noise(key, dims, scale, limit, shards=(), held_as=jnp.bfloat16):
    level = level_of(key, dims, shards, -0.22, 0.18) if shards else 1.0
    drawn = jax.random.normal(key, dims, jnp.float32) * scale * level
    return jnp.minimum(jnp.maximum(drawn, -limit), limit).astype(held_as)


def setup_inputs(seed: int = 0) -> dict:
    key_list = jax.random.split(jax.random.key(seed), 11)
    features = noise(key_list[0], (SNAPS, VERTS, D), 1.0, 6.0, ((0, 8), (1, 32)))
    tile_cols = draw_tile_cols(jax.random.fold_in(key_list[10], 71), 0)
    tile_vals = noise(key_list[2], (SNAPS, NBLK, TILES, TB, TB), (TILES * TB) ** -0.5, 0.1875, ((0, 8), (1, 32)))
    space_weight = noise(key_list[3], (D, D), D ** -0.5, 0.5)
    positions = noise(key_list[4], (SNAPS, D), 1.0, 6.0)
    attn_proj = noise(key_list[5], (D, 3 * D), D ** -0.5, 0.5)
    attn_out = noise(key_list[6], (D, D), D ** -0.5, 0.5)
    norm_gain = jnp.clip(1.0 + 0.18 * jax.random.normal(key_list[7], (D,), jnp.float32), 0.1, 1.9)
    mlp_up = noise(key_list[8], (D, FFN), D ** -0.5, 0.5)
    mlp_down = noise(key_list[9], (FFN, D), FFN ** -0.5, 0.25)
    return dict(features=features, tile_cols=tile_cols, tile_vals=tile_vals, space_weight=space_weight, positions=positions, attn_proj=attn_proj, attn_out=attn_out, norm_gain=norm_gain, mlp_up=mlp_up, mlp_down=mlp_down)


cap_value = 4.0
norm_eps = 1e-05

def spatial_snap(feature_snap, cols_snap, vals_snap, space_weight):
    grouped = feature_snap.reshape(NBLK, TB, D)
    blocks = jnp.take(grouped, cols_snap.reshape(-1), axis=0).reshape(NBLK, TILES, TB, D)
    summed = jnp.einsum('rkij,rkjd->rid', vals_snap.astype(jnp.float32), blocks.astype(jnp.float32)).astype(jnp.bfloat16)
    hidden = jax.nn.relu(jnp.dot(summed.reshape(-1, D), space_weight, preferred_element_type=jnp.float32))
    return hidden.astype(jnp.bfloat16).reshape(VERTS, D)

def temporal(hidden, positions, attn_proj, attn_out, norm_gain, mlp_up, mlp_down):
    snap_total = hidden.shape[0]
    head_dim = D // HEADS
    mixed_in = (hidden.astype(jnp.float32) + positions.astype(jnp.float32)[:, None, :]).astype(jnp.bfloat16)
    flat_in = mixed_in.reshape(-1, D)
    projected = jnp.dot(flat_in, attn_proj, preferred_element_type=jnp.float32).astype(jnp.bfloat16)
    projected = projected.reshape(snap_total, -1, 3, HEADS, head_dim)
    query_part = projected[:, :, 0].astype(jnp.float32)
    key_part = projected[:, :, 1].astype(jnp.float32)
    value_part = projected[:, :, 2].astype(jnp.float32)
    scores = jnp.einsum('tvhd,uvhd->vhtu', query_part, key_part) / math.sqrt(head_dim)
    capped = cap_value * jnp.tanh(scores / cap_value)
    causal = jnp.arange(snap_total)[:, None] >= jnp.arange(snap_total)[None, :]
    raised = jnp.where(causal, jnp.exp(capped), 0.0)
    weights = (raised / lax.optimization_barrier(jnp.sum(raised, axis=-1, keepdims=True))).astype(jnp.bfloat16)
    attended = jnp.einsum('vhtu,uvhd->tvhd', weights.astype(jnp.float32), value_part).astype(jnp.bfloat16)
    stream = flat_in.astype(jnp.float32) + jnp.dot(attended.reshape(-1, D), attn_out, preferred_element_type=jnp.float32)
    centre = lax.optimization_barrier(jnp.mean(stream, axis=-1, keepdims=True))
    spread = lax.optimization_barrier(jnp.mean((stream - centre) ** 2, axis=-1, keepdims=True))
    normed = ((stream - centre) * lax.rsqrt(spread + norm_eps) * norm_gain).astype(jnp.bfloat16)
    expanded = jax.nn.relu(jnp.dot(normed, mlp_up, preferred_element_type=jnp.float32)).astype(jnp.bfloat16)
    output = stream + jnp.dot(expanded, mlp_down, preferred_element_type=jnp.float32)
    return output.astype(jnp.bfloat16).reshape(snap_total, -1, D)

def reference(features, tile_cols, tile_vals, space_weight, positions, attn_proj, attn_out, norm_gain, mlp_up, mlp_down):
    hidden = lax.map(lambda item: spatial_snap(item[0], item[1], item[2], space_weight), (features, tile_cols, tile_vals))
    groups = VERTS // VT
    split_up = hidden.reshape(SNAPS, groups, VT, D).transpose(1, 0, 2, 3)
    result = lax.map(lambda piece: temporal(piece, positions, attn_proj, attn_out, norm_gain, mlp_up, mlp_down), split_up)
    return result.transpose(1, 0, 2, 3).reshape(SNAPS, VERTS, D)
```

```python
import functools
import math

import jax
import jax.numpy as jnp
from jax import lax
from jax.experimental import pallas as pl
from jax.experimental.pallas import tpu as pltpu
from jax.sharding import PartitionSpec as P

HEADS = 16
MESH = pl.DeviceIdType.MESH
cap_value = 4.0
norm_eps = 1e-05

ZORD = (0, 1, 7, 2, 6, 3, 5, 4)
POS = {dz: p for p, dz in enumerate(ZORD)}
GROUPS = ((0,), (1, 7), (2, 6), (3, 5), (4,))
PAIRED = (0, 1, 2)
DIRECT = (3,)


def temporal(hidden, positions, attn_proj, attn_out, norm_gain, mlp_up, mlp_down):
    snap_total = hidden.shape[0]
    feature_dim = hidden.shape[2]
    head_count = HEADS
    head_dim = feature_dim // head_count
    mixed_in = (hidden.astype(jnp.float32) + positions.astype(jnp.float32)[:, None, :]).astype(
        jnp.bfloat16
    )
    flat_in = mixed_in.reshape(-1, feature_dim)
    projected = jnp.dot(flat_in, attn_proj, preferred_element_type=jnp.float32).astype(jnp.bfloat16)
    projected = projected.reshape(snap_total, -1, 3, head_count, head_dim)
    query_part = projected[:, :, 0]
    key_part = projected[:, :, 1]
    value_part = projected[:, :, 2]
    scores = jnp.einsum(
        "tvhd,uvhd->vhtu", query_part, key_part, preferred_element_type=jnp.float32
    ) / math.sqrt(head_dim)
    capped = cap_value * jnp.tanh(scores / cap_value)
    causal = jnp.arange(snap_total)[:, None] >= jnp.arange(snap_total)[None, :]
    raised = jnp.where(causal, jnp.exp(capped), 0.0)
    weights = (raised / jnp.sum(raised, axis=-1, keepdims=True)).astype(jnp.bfloat16)
    attended = jnp.einsum(
        "vhtu,uvhd->tvhd", weights, value_part, preferred_element_type=jnp.float32
    ).astype(jnp.bfloat16)
    stream = flat_in.astype(jnp.float32) + jnp.dot(
        attended.reshape(-1, feature_dim), attn_out, preferred_element_type=jnp.float32
    )
    centre = jnp.mean(stream, axis=-1, keepdims=True)
    spread = jnp.mean((stream - centre) ** 2, axis=-1, keepdims=True)
    normed = ((stream - centre) * lax.rsqrt(spread + norm_eps) * norm_gain).astype(jnp.bfloat16)
    expanded = jax.nn.relu(jnp.dot(normed, mlp_up, preferred_element_type=jnp.float32)).astype(
        jnp.bfloat16
    )
    output = stream + jnp.dot(expanded, mlp_down, preferred_element_type=jnp.float32)
    return output.astype(jnp.bfloat16).reshape(snap_total, -1, feature_dim)


class Sems:
    def __init__(self, send, recv):
        self.send, self.recv, self.n = send, recv, 0

    def copy(self, src, dst, device):
        i = self.n
        self.n += 1
        return pltpu.make_async_remote_copy(
            src, dst, self.send.at[i], self.recv.at[i], device_id=device, device_id_type=MESH
        )


COPIES = 3 + 4 * 8 + len(PAIRED) * 9 + 5 * (4 * 2 + len(DIRECT)) + 4 * 7


def spatial_kernel(
    feat, tab_s, tab_v, slots, weight, tv_hbm, out,
    tv, tabr, tabs, stg, hid, arr, send, recv, lsem, *bufs,
):
    bufs = list(bufs)
    comp = [bufs.pop(0) for _ in range(4)]
    own = [{dz: bufs.pop(0) for dz in range(1, 8)} for _ in range(4)]
    pair = {s: {dz: bufs.pop(0) for dz in range(8)} for s in PAIRED}
    for s in range(4):
        own[s][0] = feat.at[s]

    v = lax.axis_index("vert")
    t = lax.axis_index("tm")
    z, x = v // 4, v % 4
    up = dict(vert=((z + 1) % 8) * 4 + x)
    down = dict(vert=((z + 7) % 8) * 4 + x)
    side = {k: dict(vert=z * 4 + (x + k) % 4) for k in (1, 2, 3)}
    times = {k: dict(tm=(t + k) % 8) for k in range(1, 8)}

    barrier = pltpu.get_barrier_semaphore()
    peers = [up, down] + list(side.values()) + list(times.values())
    for peer in peers:
        pl.semaphore_signal(barrier, inc=1, device_id=peer, device_id_type=MESH)
    pl.semaphore_wait(barrier, len(peers))

    sems = Sems(send, recv)
    started = []

    def go(copy):
        copy.start()
        started.append(copy)
        return copy

    def ring(buf, step):
        if step < 4:
            a = sems.copy(buf[(9 - step) % 8], buf[8 - step], up)
            b = sems.copy(buf[step - 1], buf[step], down)
        else:
            a = sems.copy(buf[5].at[0:2], buf[4].at[0:2], up)
            b = sems.copy(buf[3].at[2:4], buf[4].at[2:4], down)
        return go(a), go(b)

    tables = {k: go(sems.copy(tab_v, tabr.at[3 - k], side[k])) for k in (1, 2, 3)}
    load = pltpu.make_async_copy(tv_hbm, tv, lsem.at[0])
    load.start()
    ringed = {s: ring(own[s], 1) for s in range(4)}
    swapped = {s: go(sems.copy(feat.at[s], pair[s][0], side[2])) for s in PAIRED}
    for k in (1, 2, 3):
        tables[k].wait_recv()
    for k in (1, 2, 3):
        pltpu.make_async_copy(tabr.at[k - 1], tabs.at[k - 1], lsem.at[k]).start()
    for k in (1, 2, 3):
        pltpu.make_async_copy(tabr.at[k - 1], tabs.at[k - 1], lsem.at[k]).wait()

    stg_refs = stg
    stg = {}
    n = 0
    for s in range(4):
        for k in (1, 3) if s in PAIRED else (1, 3, 2):
            stg[s, k] = stg_refs.at[n]
            n += 1
    crossed = {s: [] for s in range(4)}

    def keep(buf, s, dx, group):
        for dz in group:
            ci = dx * 8 + POS[dz]
            for w in range(2):
                comp[s][ci * 2 + w] = buf[dz][tab_s[s, w * 32 + ci]]

    def share(s, group):
        p0 = POS[group[0]]
        rows = 2 * len(group)
        for k in (1, 3) if s in PAIRED else (1, 3, 2):
            ref = stg[s, k]
            dx = 4 - k
            for dz in group:
                for w in range(2):
                    ci = dx * 8 + POS[dz]
                    ref[POS[dz] * 2 + w] = own[s][dz][tabs[k - 1, s, w * 32 + ci]]
        keep(own[s], s, 0, group)
        for k in (1, 3) if s in PAIRED else (1, 3, 2):
            dx = 4 - k
            crossed[s].append(
                go(
                    sems.copy(
                        stg[s, k].at[2 * p0 : 2 * p0 + rows],
                        comp[s].at[dx * 16 + 2 * p0 : dx * 16 + 2 * p0 + rows],
                        side[k],
                    )
                )
            )

    for s in range(4):
        share(s, GROUPS[0])
    paired = {}
    for step in range(1, 5):
        for s in range(4):
            for c in ringed[s]:
                c.wait_recv()
            if step < 4:
                ringed[s] = ring(own[s], step + 1)
            if step == 3 and s in PAIRED:
                swapped[s].wait_recv()
                paired[s] = ring(pair[s], 1)
            share(s, GROUPS[step])
    for s in PAIRED:
        keep(pair[s], s, 2, GROUPS[0])
    for step in range(1, 5):
        for s in PAIRED:
            for c in paired[s]:
                c.wait_recv()
            if step < 4:
                paired[s] = ring(pair[s], step + 1)
            keep(pair[s], s, 2, GROUPS[step])

    load.wait()
    sent = []
    for s in DIRECT + PAIRED:
        for c in crossed[s]:
            c.wait_recv()
        for r in range(4):
            left = jnp.concatenate([tv[s, r, k] for k in range(8)], axis=1)
            right = jnp.concatenate([comp[s][slots[s, r * 8 + k]] for k in range(8)], axis=0)
            summed = jnp.dot(left, right, preferred_element_type=jnp.float32).astype(jnp.bfloat16)
            hidden = jnp.dot(summed, weight[...], preferred_element_type=jnp.float32)
            hidden = jnp.maximum(hidden, 0.0).astype(jnp.bfloat16)
            hid[s, 2 * r : 2 * r + 2] = hidden.reshape(2, 64, 128)
        arr[t * 4 + s] = hid[s, t]
        for k in range(1, 8):
            c = sems.copy(hid.at[s, (t + k) % 8], arr.at[t * 4 + s], times[k])
            sent.append(go(c))
    for c in sent:
        c.wait_recv()
    out[...] = arr[...]
    for c in started:
        c.wait_send()
    assert sems.n == COPIES


def spatial(features, tile_cols, tile_vals, space_weight):
    v = lax.axis_index("vert")
    z, x = v // 4, v % 4
    cols = tile_cols.reshape(4, 32)
    owner, blk = cols // 4, cols % 4
    dz, dx = (owner // 4 - z) % 8, (owner % 4 - x) % 4
    pos = jnp.where(dz == 0, 0, jnp.where(dz <= 4, 2 * dz - 1, 2 * (8 - dz)))
    ci = dx * 8 + pos
    hit = ci[:, :, None] == jnp.arange(32)
    low = jnp.min(jnp.where(hit, blk[:, :, None], 3), axis=1)
    high = jnp.max(jnp.where(hit, blk[:, :, None], 0), axis=1)
    mine = jnp.sum(jnp.where(hit, low[:, None, :], 0), axis=2)
    slots = ci * 2 + (blk != mine).astype(jnp.int32)
    table = jnp.pad(jnp.concatenate([low, high], axis=1), ((0, 4), (0, 64)))

    vmem = pl.BlockSpec(memory_space=pltpu.VMEM)
    smem = pl.BlockSpec(memory_space=pltpu.SMEM)
    blocks = functools.partial(pltpu.VMEM, dtype=jnp.bfloat16)
    block4 = pltpu.VMEM((4, 128, 128), jnp.bfloat16)
    stages = 2 * 4 + len(DIRECT)
    return pl.pallas_call(
        spatial_kernel,
        out_shape=jax.ShapeDtypeStruct((32, 64, 128), jnp.bfloat16),
        in_specs=[vmem, smem, vmem, smem, vmem, pl.BlockSpec(memory_space=pl.ANY)],
        out_specs=vmem,
        scratch_shapes=[
            pltpu.VMEM((4, 4, 8, 128, 128), jnp.bfloat16),
            pltpu.VMEM((3, 8, 128), jnp.int32),
            pltpu.SMEM((3, 8, 128), jnp.int32),
            pltpu.VMEM((stages, 16, 128, 128), jnp.bfloat16),
            pltpu.VMEM((4, 8, 64, 128), jnp.bfloat16),
            pltpu.VMEM((32, 64, 128), jnp.bfloat16),
            pltpu.SemaphoreType.DMA((COPIES,)),
            pltpu.SemaphoreType.DMA((COPIES,)),
            pltpu.SemaphoreType.DMA((4,)),
        ]
        + [pltpu.VMEM((64, 128, 128), jnp.bfloat16)] * 4
        + [block4] * 28
        + [block4] * (8 * len(PAIRED)),
        compiler_params=pltpu.CompilerParams(
            collective_id=0, has_side_effects=True, vmem_limit_bytes=60 * 2**20
        ),
    )(
        features.reshape(4, 4, 128, 128), table, table, slots, space_weight, tile_vals
    )


def local(
    features, tile_cols, tile_vals, space_weight, positions, attn_proj, attn_out, norm_gain,
    mlp_up, mlp_down,
):
    timeline = spatial(features, tile_cols, tile_vals, space_weight)
    result = temporal(timeline, positions, attn_proj, attn_out, norm_gain, mlp_up, mlp_down)
    result = result.reshape(32, 1, -1, 128)
    embedded = lax.all_to_all(result, "tm", split_axis=0, concat_axis=1, tiled=True)
    return embedded.reshape(4, 512, 128)


def solution(mesh):
    placed = (
        P("tm", "vert", None),
        P("tm", "vert", None),
        P("tm", "vert", None, None, None),
        P(),
        P(),
        P(),
        P(),
        P(),
        P(),
        P(),
    )
    return jax.shard_map(
        local, mesh=mesh, in_specs=placed, out_specs=P("tm", "vert", None), check_vma=False
    )
```

```python
import math

import jax
import jax.numpy as jnp
from jax import lax
from jax.experimental import pallas as pl
from jax.experimental.pallas import tpu as pltpu
from jax.sharding import PartitionSpec as P

MESH = pl.DeviceIdType.MESH
norm_eps = 1e-05
SCORE = 1.0 / (4.0 * math.sqrt(8.0))
POWER = 4.0 * math.log2(math.e)

ZORD = (0, 1, 7, 2, 6, 3, 5, 4)
POS = {dz: p for p, dz in enumerate(ZORD)}
GROUPS = ((0,), (1, 7), (2, 6), (3, 5), (4,))
PAIRED = (0, 1, 2)
DIRECT = (3,)


def dot_t(a, b):
    return lax.dot_general(a, b, (((1,), (1,)), ((), ())), preferred_element_type=jnp.float32)


def dot(a, b):
    return jnp.dot(a, b, preferred_element_type=jnp.float32)


def arrange(attn_proj, attn_out, wcat, wout):
    row = lax.broadcasted_iota(jnp.int32, (192, 384), 0)
    col = lax.broadcasted_iota(jnp.int32, (192, 384), 1)
    base = (row // 64) * 128 + (row % 8) * 8 + (row // 8) % 8
    for half in range(2):
        pick = (col == base + half * 64).astype(jnp.bfloat16)
        wcat[:, half * 128 : (half + 1) * 128] = dot_t(pick, attn_proj[...]).astype(jnp.bfloat16)
    row = lax.broadcasted_iota(jnp.int32, (64, 128), 0)
    col = lax.broadcasted_iota(jnp.int32, (64, 128), 1)
    base = (row % 8) * 8 + row // 8
    for half in range(2):
        pick = (col == base + half * 64).astype(jnp.bfloat16)
        wout[:, half * 128 : (half + 1) * 128] = dot(pick, attn_out[...]).astype(jnp.bfloat16)


def project(t0, t1, arr, pos, wcat, mix, proj):
    zero = jnp.zeros((64, 128), jnp.bfloat16)
    rows = []
    for t in (t0, t1):
        m = (arr[t].astype(jnp.float32) + pos[t].astype(jnp.float32)).astype(jnp.bfloat16)
        mix[t] = m
        rows.append(jnp.concatenate([m, zero], axis=1))
        rows.append(jnp.concatenate([zero, m], axis=1))
    both = jnp.concatenate(rows, axis=0)
    p = dot_t(wcat[...], both).astype(jnp.bfloat16).astype(jnp.float32)
    for i, t in enumerate((t0, t1)):
        q = p[:, i * 128 : (i + 1) * 128]
        proj[t, 0:64] = q[0:64] * SCORE
        proj[t, 64:192] = q[64:192]


def attend(tb, proj, att):
    def parts(t, k):
        return proj[t, 64 * k : 64 * (k + 1)].reshape(8, 8, 128)

    for pair in range(2):
        qs = [parts(4 * tb + 2 * pair + i, 0) for i in range(2)]

        def quad(uq, carry, diag):
            carry = list(carry)
            for ui in range(4):
                if diag and ui > 2 * pair + 1:
                    continue
                u = 4 * uq + ui
                k, v = parts(u, 1), parts(u, 2)
                for i in range(2):
                    if diag and ui > 2 * pair + i:
                        continue
                    e = jnp.exp2(POWER * jnp.tanh(jnp.sum(qs[i] * k, axis=0)))
                    carry[2 * i] = carry[2 * i] + e[None] * v
                    carry[2 * i + 1] = carry[2 * i + 1] + e
            return tuple(carry)

        zero = (jnp.zeros((8, 8, 128), jnp.float32), jnp.zeros((8, 128), jnp.float32)) * 2
        carry = lax.fori_loop(0, tb, lambda uq, c: quad(uq, c, False), zero)
        carry = quad(tb, carry, True)
        for i in range(2):
            a = carry[2 * i] * (1.0 / carry[2 * i + 1])[None]
            att[2 * pair + i] = a.reshape(64, 128)


def finish(tb, att, mix, wout, gain, mlp_up, mlp_down):
    rows = jnp.concatenate([att[i].T for i in range(4)], axis=0).astype(jnp.bfloat16)
    o = dot(rows, wout[...])
    out = jnp.concatenate(
        [o[128 * i : 128 * i + 64, 0:128] + o[128 * i + 64 : 128 * i + 128, 128:256] for i in range(4)],
        axis=0,
    )
    m = mix[pl.ds(4 * tb, 4)].reshape(256, 128)
    stream = m.astype(jnp.float32) + out
    centre = jnp.mean(stream, axis=-1, keepdims=True)
    shifted = stream - centre
    spread = jnp.mean(shifted * shifted, axis=-1, keepdims=True)
    normed = (shifted * lax.rsqrt(spread + norm_eps) * gain[...]).astype(jnp.bfloat16)
    expanded = jnp.maximum(dot(normed, mlp_up[...]), 0.0).astype(jnp.bfloat16)
    return (stream + dot(expanded, mlp_down[...])).astype(jnp.bfloat16).reshape(4, 64, 128)


class Sems:
    def __init__(self, send, recv):
        self.send, self.recv, self.n = send, recv, 0

    def copy(self, src, dst, device):
        i = self.n
        self.n += 1
        return pltpu.make_async_remote_copy(
            src, dst, self.send.at[i], self.recv.at[i], device_id=device, device_id_type=MESH
        )


COPIES = 3 + 4 * 8 + len(PAIRED) * 9 + 5 * (4 * 2 + len(DIRECT)) + 4 * 7 + 7


def kernel(
    feat, tab_s, tab_v, slots, weight, tv_hbm, positions, attn_proj, attn_out, gain, mlp_up,
    mlp_down, out,
    tv, tabr, tabs, stg, hid, arr, wcat, wout, pos, mix, proj, att, obuf, oarr, send, recv, lsem,
    *bufs,
):
    bufs = list(bufs)
    comp = [bufs.pop(0) for _ in range(4)]
    own = [{dz: bufs.pop(0) for dz in range(1, 8)} for _ in range(4)]
    pair = {s: {dz: bufs.pop(0) for dz in range(8)} for s in PAIRED}
    for s in range(4):
        own[s][0] = feat.at[s]

    v = lax.axis_index("vert")
    t = lax.axis_index("tm")
    z, x = v // 4, v % 4
    up = dict(vert=((z + 1) % 8) * 4 + x)
    down = dict(vert=((z + 7) % 8) * 4 + x)
    side = {k: dict(vert=z * 4 + (x + k) % 4) for k in (1, 2, 3)}
    times = {k: dict(tm=(t + k) % 8) for k in range(1, 8)}

    barrier = pltpu.get_barrier_semaphore()
    peers = [up, down] + list(side.values()) + list(times.values())
    for peer in peers:
        pl.semaphore_signal(barrier, inc=1, device_id=peer, device_id_type=MESH)
    pl.semaphore_wait(barrier, len(peers))

    sems = Sems(send, recv)
    started = []

    def go(copy):
        copy.start()
        started.append(copy)
        return copy

    def ring(buf, step):
        if step < 4:
            a = sems.copy(buf[(9 - step) % 8], buf[8 - step], up)
            b = sems.copy(buf[step - 1], buf[step], down)
        else:
            a = sems.copy(buf[5].at[0:2], buf[4].at[0:2], up)
            b = sems.copy(buf[3].at[2:4], buf[4].at[2:4], down)
        return go(a), go(b)

    tables = {k: go(sems.copy(tab_v, tabr.at[3 - k], side[k])) for k in (1, 2, 3)}
    load = pltpu.make_async_copy(tv_hbm, tv, lsem.at[0])
    load.start()
    ringed = {s: ring(own[s], 1) for s in range(4)}
    swapped = {s: go(sems.copy(feat.at[s], pair[s][0], side[2])) for s in PAIRED}
    for k in (1, 2, 3):
        tables[k].wait_recv()
    for k in (1, 2, 3):
        pltpu.make_async_copy(tabr.at[k - 1], tabs.at[k - 1], lsem.at[k]).start()
    for k in (1, 2, 3):
        pltpu.make_async_copy(tabr.at[k - 1], tabs.at[k - 1], lsem.at[k]).wait()

    stg_refs = stg
    stg = {}
    n = 0
    for s in range(4):
        for k in (1, 3) if s in PAIRED else (1, 3, 2):
            stg[s, k] = stg_refs.at[n]
            n += 1
    arrange(attn_proj, attn_out, wcat, wout)
    pos[...] = positions[...].astype(jnp.float32).reshape(32, 1, 128)
    crossed = {s: [] for s in range(4)}

    def keep(buf, s, dx, group):
        for dz in group:
            ci = dx * 8 + POS[dz]
            for w in range(2):
                comp[s][ci * 2 + w] = buf[dz][tab_s[s, w * 32 + ci]]

    def share(s, group):
        p0 = POS[group[0]]
        rows = 2 * len(group)
        for k in (1, 3) if s in PAIRED else (1, 3, 2):
            ref = stg[s, k]
            dx = 4 - k
            for dz in group:
                for w in range(2):
                    ci = dx * 8 + POS[dz]
                    ref[POS[dz] * 2 + w] = own[s][dz][tabs[k - 1, s, w * 32 + ci]]
        keep(own[s], s, 0, group)
        for k in (1, 3) if s in PAIRED else (1, 3, 2):
            dx = 4 - k
            crossed[s].append(
                go(
                    sems.copy(
                        stg[s, k].at[2 * p0 : 2 * p0 + rows],
                        comp[s].at[dx * 16 + 2 * p0 : dx * 16 + 2 * p0 + rows],
                        side[k],
                    )
                )
            )

    for s in range(4):
        share(s, GROUPS[0])
    paired = {}
    for step in range(1, 5):
        for s in range(4):
            for c in ringed[s]:
                c.wait_recv()
            if step < 4:
                ringed[s] = ring(own[s], step + 1)
            if step == 3 and s in PAIRED:
                swapped[s].wait_recv()
                paired[s] = ring(pair[s], 1)
            share(s, GROUPS[step])
    for s in PAIRED:
        keep(pair[s], s, 2, GROUPS[0])
    for step in range(1, 5):
        for s in PAIRED:
            for c in paired[s]:
                c.wait_recv()
            if step < 4:
                paired[s] = ring(pair[s], step + 1)
            keep(pair[s], s, 2, GROUPS[step])

    load.wait()
    sent = []
    for s in DIRECT + PAIRED:
        for c in crossed[s]:
            c.wait_recv()
        for r in range(4):
            left = jnp.concatenate([tv[s, r, k] for k in range(8)], axis=1)
            right = jnp.concatenate([comp[s][slots[s, r * 8 + k]] for k in range(8)], axis=0)
            summed = jnp.dot(left, right, preferred_element_type=jnp.float32).astype(jnp.bfloat16)
            hidden = jnp.dot(summed, weight[...], preferred_element_type=jnp.float32)
            hidden = jnp.maximum(hidden, 0.0).astype(jnp.bfloat16)
            hid[s, 2 * r : 2 * r + 2] = hidden.reshape(2, 64, 128)
        arr[t * 4 + s] = hid[s, t]
        for k in range(1, 8):
            c = sems.copy(hid.at[s, (t + k) % 8], arr.at[t * 4 + s], times[k])
            sent.append(go(c))
    for c in sent:
        c.wait_recv()

    @pl.loop(0, 16)
    def _(i):
        project(2 * i, 2 * i + 1, arr, pos, wcat, mix, proj)

    def back(j):
        return pltpu.make_async_remote_copy(
            obuf.at[j], oarr.at[:, t], send.at[sems.n + j], recv.at[sems.n + j],
            device_id=dict(tm=(t + 1 + j) % 8), device_id_type=MESH,
        )

    @pl.loop(0, 7)
    def _(j):
        tb = (t + 1 + j) % 8
        attend(tb, proj, att)
        obuf[j] = finish(tb, att, mix, wout, gain, mlp_up, mlp_down)
        back(j).start()

    attend(t, proj, att)
    oarr[:, t] = finish(t, att, mix, wout, gain, mlp_up, mlp_down)

    @pl.loop(0, 7)
    def _(j):
        back(j).wait_recv()

    out[...] = oarr[...]

    @pl.loop(0, 7)
    def _(j):
        back(j).wait_send()

    for c in started:
        c.wait_send()
    assert sems.n + 7 == COPIES


def local(
    features, tile_cols, tile_vals, space_weight, positions, attn_proj, attn_out, norm_gain,
    mlp_up, mlp_down,
):
    v = lax.axis_index("vert")
    z, x = v // 4, v % 4
    cols = tile_cols.reshape(4, 32)
    owner, blk = cols // 4, cols % 4
    dz, dx = (owner // 4 - z) % 8, (owner % 4 - x) % 4
    pos = jnp.where(dz == 0, 0, jnp.where(dz <= 4, 2 * dz - 1, 2 * (8 - dz)))
    ci = dx * 8 + pos
    hit = ci[:, :, None] == jnp.arange(32)
    low = jnp.min(jnp.where(hit, blk[:, :, None], 3), axis=1)
    high = jnp.max(jnp.where(hit, blk[:, :, None], 0), axis=1)
    mine = jnp.sum(jnp.where(hit, low[:, None, :], 0), axis=2)
    slots = ci * 2 + (blk != mine).astype(jnp.int32)
    table = jnp.pad(jnp.concatenate([low, high], axis=1), ((0, 4), (0, 64)))

    vmem = pl.BlockSpec(memory_space=pltpu.VMEM)
    smem = pl.BlockSpec(memory_space=pltpu.SMEM)
    block4 = pltpu.VMEM((4, 128, 128), jnp.bfloat16)
    stages = 2 * 4 + len(DIRECT)
    embedded = pl.pallas_call(
        kernel,
        out_shape=jax.ShapeDtypeStruct((4, 8, 64, 128), jnp.bfloat16),
        in_specs=[vmem, smem, vmem, smem, vmem, pl.BlockSpec(memory_space=pl.ANY)] + [vmem] * 6,
        out_specs=vmem,
        scratch_shapes=[
            pltpu.VMEM((4, 4, 8, 128, 128), jnp.bfloat16),
            pltpu.VMEM((3, 8, 128), jnp.int32),
            pltpu.SMEM((3, 8, 128), jnp.int32),
            pltpu.VMEM((stages, 16, 128, 128), jnp.bfloat16),
            pltpu.VMEM((4, 8, 64, 128), jnp.bfloat16),
            pltpu.VMEM((32, 64, 128), jnp.bfloat16),
            pltpu.VMEM((192, 256), jnp.bfloat16),
            pltpu.VMEM((64, 256), jnp.bfloat16),
            pltpu.VMEM((32, 1, 128), jnp.float32),
            pltpu.VMEM((32, 64, 128), jnp.bfloat16),
            pltpu.VMEM((32, 192, 128), jnp.float32),
            pltpu.VMEM((4, 64, 128), jnp.float32),
            pltpu.VMEM((7, 4, 64, 128), jnp.bfloat16),
            pltpu.VMEM((4, 8, 64, 128), jnp.bfloat16),
            pltpu.SemaphoreType.DMA((COPIES,)),
            pltpu.SemaphoreType.DMA((COPIES,)),
            pltpu.SemaphoreType.DMA((4,)),
        ]
        + [pltpu.VMEM((64, 128, 128), jnp.bfloat16)] * 4
        + [block4] * 28
        + [block4] * (8 * len(PAIRED)),
        compiler_params=pltpu.CompilerParams(
            collective_id=0, has_side_effects=True, vmem_limit_bytes=60 * 2**20
        ),
    )(
        features.reshape(4, 4, 128, 128), table, table, slots, space_weight, tile_vals,
        positions, attn_proj, attn_out, norm_gain.reshape(1, 128), mlp_up, mlp_down,
    )
    return embedded.reshape(4, 512, 128)


def solution(mesh):
    placed = (
        P("tm", "vert", None),
        P("tm", "vert", None),
        P("tm", "vert", None, None, None),
        P(),
        P(),
        P(),
        P(),
        P(),
        P(),
        P(),
    )
    return jax.shard_map(
        local, mesh=mesh, in_specs=placed, out_specs=P("tm", "vert", None), check_vma=False
    )
```

```python
import math

import jax
import jax.numpy as jnp
from jax import lax
from jax.experimental import pallas as pl
from jax.experimental.pallas import tpu as pltpu
from jax.sharding import PartitionSpec as P

MESH = pl.DeviceIdType.MESH
norm_eps = 1e-05
SCORE = 1.0 / (4.0 * math.sqrt(8.0))
POWER = 4.0 * math.log2(math.e)

ZORD = (0, 1, 7, 2, 6, 3, 5, 4)
POS = {dz: p for p, dz in enumerate(ZORD)}
GROUPS = ((0,), (1, 7), (2, 6), (3, 5), (4,))
PAIRED = (0, 1, 2)
DIRECT = (3,)
EARLY, LATE = (0,), (1, 2)
ORDER = (3, 0, 1, 2)


def dot_t(a, b):
    return lax.dot_general(a, b, (((1,), (1,)), ((), ())), preferred_element_type=jnp.float32)


def dot(a, b):
    return jnp.dot(a, b, preferred_element_type=jnp.float32)


def arrange(attn_proj, attn_out, wcat, wout):
    row = lax.broadcasted_iota(jnp.int32, (192, 384), 0)
    col = lax.broadcasted_iota(jnp.int32, (192, 384), 1)
    base = (row // 64) * 128 + (row % 8) * 8 + (row // 8) % 8
    for half in range(2):
        pick = (col == base + half * 64).astype(jnp.bfloat16)
        wcat[:, half * 128 : (half + 1) * 128] = dot_t(pick, attn_proj[...]).astype(jnp.bfloat16)
    row = lax.broadcasted_iota(jnp.int32, (64, 128), 0)
    col = lax.broadcasted_iota(jnp.int32, (64, 128), 1)
    base = (row % 8) * 8 + row // 8
    for half in range(2):
        pick = (col == base + half * 64).astype(jnp.bfloat16)
        wout[:, half * 128 : (half + 1) * 128] = dot(pick, attn_out[...]).astype(jnp.bfloat16)


def project(t0, t1, arr, pos, wcat, mix, proj):
    zero = jnp.zeros((64, 128), jnp.bfloat16)
    rows = []
    for t in (t0, t1):
        m = (arr[t].astype(jnp.float32) + pos[t]).astype(jnp.bfloat16)
        mix[t] = m
        rows.append(jnp.concatenate([m, zero], axis=1))
        rows.append(jnp.concatenate([zero, m], axis=1))
    both = jnp.concatenate(rows, axis=0)
    p = dot_t(wcat[...], both).astype(jnp.bfloat16).astype(jnp.float32)
    for i, t in enumerate((t0, t1)):
        q = p[:, i * 128 : (i + 1) * 128]
        proj[t, 0:64] = q[0:64] * SCORE
        proj[t, 64:192] = q[64:192]


def attend(tb, proj, att, slot=0):
    def parts(t, k):
        return proj[t, 64 * k : 64 * (k + 1)].reshape(8, 8, 128)

    for pair in range(2):
        qs = [parts(4 * tb + 2 * pair + i, 0) for i in range(2)]

        def quad(uq, carry, diag):
            carry = list(carry)
            for ui in range(4):
                if diag and ui > 2 * pair + 1:
                    continue
                u = 4 * uq + ui
                k, v = parts(u, 1), parts(u, 2)
                for i in range(2):
                    if diag and ui > 2 * pair + i:
                        continue
                    e = jnp.exp2(POWER * jnp.tanh(jnp.sum(qs[i] * k, axis=0)))
                    carry[2 * i] = carry[2 * i] + e[None] * v
                    carry[2 * i + 1] = carry[2 * i + 1] + e
            return tuple(carry)

        zero = (jnp.zeros((8, 8, 128), jnp.float32), jnp.zeros((8, 128), jnp.float32)) * 2
        carry = lax.fori_loop(0, tb, lambda uq, c: quad(uq, c, False), zero)
        carry = quad(tb, carry, True)
        for i in range(2):
            a = carry[2 * i] * (1.0 / carry[2 * i + 1])[None]
            att[slot + 2 * pair + i] = a.reshape(64, 128)


def finish(blocks, att, mix, wout, gain, mlp_up, mlp_down):
    n = 4 * len(blocks)
    rows = jnp.concatenate([att[i].T for i in range(n)], axis=0).astype(jnp.bfloat16)
    o = dot(rows, wout[...])
    out = jnp.concatenate(
        [o[128 * i : 128 * i + 64, 0:128] + o[128 * i + 64 : 128 * i + 128, 128:256] for i in range(n)],
        axis=0,
    )
    m = jnp.concatenate([mix[pl.ds(4 * tb, 4)].reshape(256, 128) for tb in blocks], axis=0)
    stream = m.astype(jnp.float32) + out
    centre = jnp.mean(stream, axis=-1, keepdims=True)
    shifted = stream - centre
    spread = jnp.mean(shifted * shifted, axis=-1, keepdims=True)
    normed = (shifted * lax.rsqrt(spread + norm_eps) * gain[...]).astype(jnp.bfloat16)
    expanded = jnp.maximum(dot(normed, mlp_up[...]), 0.0).astype(jnp.bfloat16)
    done = (stream + dot(expanded, mlp_down[...])).astype(jnp.bfloat16)
    return done.reshape(len(blocks), 4, 64, 128)


def index_tables(z, x, cols, tab_v, slots_v):
    c = cols[...]
    lane = lax.broadcasted_iota(jnp.int32, (4, 4, 128), 2)
    tab = jnp.where(lane < 32, 3, 0)
    seen = []
    for k in range(8):
        ck = jnp.broadcast_to(c[:, :, k : k + 1], (4, 4, 128))
        blk = ck & 3
        dz = ((ck >> 4) - z) & 7
        dx = ((ck >> 2) - x) & 3
        pos = jnp.where(dz == 0, 0, jnp.where(dz <= 4, 2 * dz - 1, 16 - 2 * dz))
        ci = dx * 8 + pos
        seen.append((blk, ci))
        tab = jnp.where(
            ci == lane,
            jnp.minimum(tab, blk),
            jnp.where(ci + 32 == lane, jnp.maximum(tab, blk), tab),
        )
    low = jnp.min(tab, axis=1, keepdims=True)
    high = jnp.max(tab, axis=1, keepdims=True)
    tab = jnp.where(lane[:, 0:1] < 32, low, high)
    tab_v[...] = jnp.zeros((8, 128), jnp.int32)
    for s in range(4):
        tab_v[s : s + 1] = tab[s]
    slots = jnp.zeros((4, 4, 128), jnp.int32)
    for k, (blk, ci) in enumerate(seen):
        mine = jnp.sum(
            jnp.where(ci == lane, tab.astype(jnp.float32), 0.0), axis=2, keepdims=True
        )
        other = (blk.astype(jnp.float32) != mine).astype(jnp.int32)
        slots = jnp.where(lane == k, 2 * ci + other, slots)
    slots_v[...] = jnp.zeros((4, 8, 128), jnp.int32)
    slots_v[:, 0:4] = slots


class Sems:
    def __init__(self, send, recv):
        self.send, self.recv, self.n = send, recv, 0

    def copy(self, src, dst, device):
        i = self.n
        self.n += 1
        return pltpu.make_async_remote_copy(
            src, dst, self.send.at[i], self.recv.at[i], device_id=device, device_id_type=MESH
        )


COPIES = 3 + 4 * 8 + len(PAIRED) * 9 + 5 * (4 * 2 + len(DIRECT)) + 4 * 7 + 7


def kernel(
    feat_h, cols_h, tv_h, weight_h, positions_h, attn_proj_h, attn_out_h, gain_h, mlp_up_h,
    mlp_down_h, out,
    feat, cols, tv, weight, positions, attn_proj, attn_out, gain, mlp_up, mlp_down,
    tab_v, slots_v, tab_s, slots, tabr, tabs, stg_refs, hid, arr, wcat, wout, pos, mix, proj, att,
    obuf, oarr, send, recv, lsem, *bufs,
):
    bufs = list(bufs)
    comp = [bufs.pop(0) for _ in range(4)]
    own = [{dz: bufs.pop(0) for dz in range(1, 8)} for _ in range(4)]
    pair = {s: {dz: bufs.pop(0) for dz in range(8)} for s in PAIRED}
    for s in range(4):
        own[s][0] = feat.at[s]
    kinds = {s: (1, 3) if s in PAIRED else (1, 3, 2) for s in range(4)}
    stg = {}
    for s in range(4):
        for k in kinds[s]:
            stg[s, k] = stg_refs.at[len(stg)]

    v = lax.axis_index("vert")
    t = lax.axis_index("tm")
    z, x = v // 4, v % 4
    up = dict(vert=((z + 1) % 8) * 4 + x)
    down = dict(vert=((z + 7) % 8) * 4 + x)
    side = {k: dict(vert=z * 4 + (x + k) % 4) for k in (1, 2, 3)}
    times = {k: dict(tm=(t + k) % 8) for k in range(1, 8)}

    barrier = pltpu.get_barrier_semaphore()
    peers = [up, down] + list(side.values()) + list(times.values())
    for peer in peers:
        pl.semaphore_signal(barrier, inc=1, device_id=peer, device_id_type=MESH)

    loads = [
        pltpu.make_async_copy(src, dst, lsem.at[i])
        for i, (src, dst) in enumerate(
            [
                (cols_h, cols), (feat_h, feat), (attn_proj_h, attn_proj), (attn_out_h, attn_out),
                (positions_h, positions), (weight_h, weight), (gain_h, gain), (mlp_up_h, mlp_up),
                (mlp_down_h, mlp_down), (tv_h, tv),
            ]
        )
    ]
    for c in loads:
        c.start()
    loads[0].wait()
    index_tables(z, x, cols, tab_v, slots_v)
    loads[1].wait()
    pl.semaphore_wait(barrier, len(peers))

    sems = Sems(send, recv)
    started = []

    def go(copy):
        copy.start()
        started.append(copy)
        return copy

    def ring(buf, step):
        if step < 4:
            a = sems.copy(buf[(9 - step) % 8], buf[8 - step], up)
            b = sems.copy(buf[step - 1], buf[step], down)
        else:
            a = sems.copy(buf[5].at[0:2], buf[4].at[0:2], up)
            b = sems.copy(buf[3].at[2:4], buf[4].at[2:4], down)
        return go(a), go(b)

    ringed = {}
    ringed[ORDER[0]] = ring(own[ORDER[0]], 1)
    tables = {k: go(sems.copy(tab_v, tabr.at[3 - k], side[k])) for k in (1, 2, 3)}
    for s in ORDER[1:]:
        ringed[s] = ring(own[s], 1)
    swapped = {s: go(sems.copy(feat.at[s], pair[s][0], side[2])) for s in PAIRED}
    for c in loads[2:]:
        c.wait()
    mine = [
        pltpu.make_async_copy(tab_v, tab_s, lsem.at[0]),
        pltpu.make_async_copy(slots_v, slots, lsem.at[1]),
    ]
    for c in mine:
        c.start()
    arrange(attn_proj, attn_out, wcat, wout)
    pos[...] = positions[...].astype(jnp.float32).reshape(32, 1, 128)
    for c in mine:
        c.wait()
    for k in (1, 2, 3):
        tables[k].wait_recv()
    theirs = [pltpu.make_async_copy(tabr.at[k], tabs.at[k], lsem.at[2 + k]) for k in range(3)]
    for c in theirs:
        c.start()
    for c in theirs:
        c.wait()

    crossed = {s: [] for s in range(4)}

    def keep(buf, s, dx, group):
        for dz in group:
            ci = dx * 8 + POS[dz]
            for w in range(2):
                comp[s][ci * 2 + w] = buf[dz][tab_s[s, w * 32 + ci]]

    def share(s, group):
        p0 = POS[group[0]]
        rows = 2 * len(group)
        for k in kinds[s]:
            for dz in group:
                for w in range(2):
                    ci = (4 - k) * 8 + POS[dz]
                    stg[s, k][POS[dz] * 2 + w] = own[s][dz][tabs[k - 1, s, w * 32 + ci]]
        keep(own[s], s, 0, group)
        for k in kinds[s]:
            q = (4 - k) * 16 + 2 * p0
            crossed[s].append(
                go(
                    sems.copy(
                        stg[s, k].at[2 * p0 : 2 * p0 + rows], comp[s].at[q : q + rows], side[k]
                    )
                )
            )

    sent = {}

    def spatial(s):
        for c in crossed[s]:
            c.wait_recv()
        for r in range(4):
            left = jnp.concatenate([tv[s, r, k] for k in range(8)], axis=1)
            right = jnp.concatenate([comp[s][slots[s, r, k]] for k in range(8)], axis=0)
            summed = dot(left, right).astype(jnp.bfloat16)
            hidden = jnp.maximum(dot(summed, weight[...]), 0.0).astype(jnp.bfloat16)
            hid[s, 2 * r : 2 * r + 2] = hidden.reshape(2, 64, 128)
        arr[t * 4 + s] = hid[s, t]
        sent[s] = [
            go(sems.copy(hid.at[s, (t + k) % 8], arr.at[t * 4 + s], times[k]))
            for k in range(1, 8)
        ]

    for s in ORDER:
        share(s, GROUPS[0])
    paired = {}
    for s in EARLY:
        swapped[s].wait_recv()
        paired[s] = ring(pair[s], 1)
    for step in range(1, 5):
        for s in ORDER:
            for c in ringed[s]:
                c.wait_recv()
            if step < 4:
                ringed[s] = ring(own[s], step + 1)
            share(s, GROUPS[step])
        for s in EARLY:
            for c in paired[s]:
                c.wait_recv()
            if step < 4:
                paired[s] = ring(pair[s], step + 1)
            if step == 1:
                keep(pair[s], s, 2, GROUPS[0])
            keep(pair[s], s, 2, GROUPS[step])
        if step == 3:
            for s in LATE:
                swapped[s].wait_recv()
                paired[s] = ring(pair[s], 1)
    for s in LATE:
        keep(pair[s], s, 2, GROUPS[0])
    for step in range(1, 4):
        for s in LATE:
            for c in paired[s]:
                c.wait_recv()
            paired[s] = ring(pair[s], step + 1)
            keep(pair[s], s, 2, GROUPS[step])
    for s in DIRECT + EARLY:
        spatial(s)
    for s in LATE:
        for c in paired[s]:
            c.wait_recv()
        keep(pair[s], s, 2, GROUPS[4])
        spatial(s)
    for s in DIRECT + EARLY + LATE:
        for c in sent[s]:
            c.wait_recv()
        for i in range(4):
            project(8 * i + s, 8 * i + 4 + s, arr, pos, wcat, mix, proj)

    def back(j):
        return pltpu.make_async_remote_copy(
            obuf.at[j], oarr.at[:, t], send.at[sems.n + j], recv.at[sems.n + j],
            device_id=dict(tm=(t + 1 + j) % 8), device_id_type=MESH,
        )

    @pl.loop(0, 3)
    def _(g):
        blocks = [(t + 1 + 2 * g + i) % 8 for i in range(2)]
        for i, tb in enumerate(blocks):
            attend(tb, proj, att, 4 * i)
        obuf[pl.ds(2 * g, 2)] = finish(blocks, att, mix, wout, gain, mlp_up, mlp_down)
        for i in range(2):
            back(2 * g + i).start()

    attend((t + 7) % 8, proj, att)
    obuf[6:7] = finish([(t + 7) % 8], att, mix, wout, gain, mlp_up, mlp_down)
    back(6).start()
    attend(t, proj, att)
    oarr[:, t] = finish([t], att, mix, wout, gain, mlp_up, mlp_down)[0]

    for c in started:
        c.wait_send()

    @pl.loop(0, 7)
    def _(j):
        back(j).wait_recv()

    out[...] = oarr[...]

    @pl.loop(0, 7)
    def _(j):
        back(j).wait_send()

    assert sems.n + 7 == COPIES


def local(
    features, tile_cols, tile_vals, space_weight, positions, attn_proj, attn_out, norm_gain,
    mlp_up, mlp_down,
):
    half, word, single = jnp.bfloat16, jnp.int32, jnp.float32
    block4 = pltpu.VMEM((4, 128, 128), half)
    embedded = pl.pallas_call(
        kernel,
        out_shape=jax.ShapeDtypeStruct((4, 8, 64, 128), half),
        in_specs=[pl.BlockSpec(memory_space=pltpu.HBM)] * 10,
        out_specs=pl.BlockSpec(memory_space=pltpu.VMEM),
        scratch_shapes=[
            pltpu.VMEM((4, 4, 128, 128), half),
            pltpu.VMEM((4, 4, 8), word),
            pltpu.VMEM((4, 4, 8, 128, 128), half),
            pltpu.VMEM((128, 128), half),
            pltpu.VMEM((32, 128), half),
            pltpu.VMEM((128, 384), half),
            pltpu.VMEM((128, 128), half),
            pltpu.VMEM((1, 128), single),
            pltpu.VMEM((128, 512), half),
            pltpu.VMEM((512, 128), half),
            pltpu.VMEM((8, 128), word),
            pltpu.VMEM((4, 8, 128), word),
            pltpu.SMEM((8, 128), word),
            pltpu.SMEM((4, 8, 128), word),
            pltpu.VMEM((3, 8, 128), word),
            pltpu.SMEM((3, 8, 128), word),
            pltpu.VMEM((2 * 4 + len(DIRECT), 16, 128, 128), half),
            pltpu.VMEM((4, 8, 64, 128), half),
            pltpu.VMEM((32, 64, 128), half),
            pltpu.VMEM((192, 256), half),
            pltpu.VMEM((64, 256), half),
            pltpu.VMEM((32, 1, 128), single),
            pltpu.VMEM((32, 64, 128), half),
            pltpu.VMEM((32, 192, 128), single),
            pltpu.VMEM((8, 64, 128), single),
            pltpu.VMEM((7, 4, 64, 128), half),
            pltpu.VMEM((4, 8, 64, 128), half),
            pltpu.SemaphoreType.DMA((COPIES,)),
            pltpu.SemaphoreType.DMA((COPIES,)),
            pltpu.SemaphoreType.DMA((10,)),
        ]
        + [pltpu.VMEM((64, 128, 128), half)] * 4
        + [block4] * 28
        + [block4] * (8 * len(PAIRED)),
        compiler_params=pltpu.CompilerParams(
            collective_id=0, has_side_effects=True, vmem_limit_bytes=44 * 2**20
        ),
    )(
        *[
            pltpu.with_memory_space_constraint(a, pltpu.HBM)
            for a in (
                features.reshape(4, 4, 128, 128), tile_cols, tile_vals, space_weight, positions,
                attn_proj, attn_out, norm_gain.reshape(1, 128), mlp_up, mlp_down,
            )
        ]
    )
    return embedded.reshape(4, 512, 128)


def solution(mesh):
    placed = (
        P("tm", "vert", None),
        P("tm", "vert", None),
        P("tm", "vert", None, None, None),
        P(),
        P(),
        P(),
        P(),
        P(),
        P(),
        P(),
    )
    return jax.shard_map(
        local, mesh=mesh, in_specs=placed, out_specs=P("tm", "vert", None), check_vma=False
    )
```

```python
import math

import jax
import jax.numpy as jnp
from jax import lax
from jax.experimental import pallas as pl
from jax.experimental.pallas import tpu as pltpu
from jax.sharding import PartitionSpec as P

MESH = pl.DeviceIdType.MESH
norm_eps = 1e-05
SCORE = 1.0 / (4.0 * math.sqrt(8.0))
POWER = 4.0 * math.log2(math.e)

ZORD = (0, 1, 7, 2, 6, 3, 5, 4)
POS = {dz: p for p, dz in enumerate(ZORD)}
GROUPS = ((0,), (1, 7), (2, 6), (3, 5), (4,))
PAIRED = (0, 1, 2)
DIRECT = (3,)
EARLY, LATE = (0,), (1, 2)
ORDER = (3, 0, 1, 2)
TABLE = {(0, 1): 0, (0, 2): 1, (0, 3): 2, (1, 0): 3, (2, 0): 4, (7, 0): 5, (6, 0): 6}


def dot_t(a, b):
    return lax.dot_general(a, b, (((1,), (1,)), ((), ())), preferred_element_type=jnp.float32)


def dot(a, b):
    return jnp.dot(a, b, preferred_element_type=jnp.float32)


def arrange(attn_proj, attn_out, wcat, wout):
    row = lax.broadcasted_iota(jnp.int32, (192, 384), 0)
    col = lax.broadcasted_iota(jnp.int32, (192, 384), 1)
    base = (row // 64) * 128 + (row % 8) * 8 + (row // 8) % 8
    for half in range(2):
        pick = (col == base + half * 64).astype(jnp.bfloat16)
        wcat[:, half * 128 : (half + 1) * 128] = dot_t(pick, attn_proj[...]).astype(jnp.bfloat16)
    row = lax.broadcasted_iota(jnp.int32, (64, 128), 0)
    col = lax.broadcasted_iota(jnp.int32, (64, 128), 1)
    base = (row % 8) * 8 + row // 8
    for half in range(2):
        pick = (col == base + half * 64).astype(jnp.bfloat16)
        wout[:, half * 128 : (half + 1) * 128] = dot(pick, attn_out[...]).astype(jnp.bfloat16)


def project(t0, t1, arr, pos, wcat, mix, proj):
    zero = jnp.zeros((64, 128), jnp.bfloat16)
    rows = []
    for t in (t0, t1):
        m = (arr[t].astype(jnp.float32) + pos[t]).astype(jnp.bfloat16)
        mix[t] = m
        rows.append(jnp.concatenate([m, zero], axis=1))
        rows.append(jnp.concatenate([zero, m], axis=1))
    both = jnp.concatenate(rows, axis=0)
    p = dot_t(wcat[...], both).astype(jnp.bfloat16).astype(jnp.float32)
    for i, t in enumerate((t0, t1)):
        q = p[:, i * 128 : (i + 1) * 128]
        proj[t, 0:64] = q[0:64] * SCORE
        proj[t, 64:192] = q[64:192]


def attend(tb, proj, att, slot=0):
    def parts(t, k):
        return proj[t, 64 * k : 64 * (k + 1)].reshape(8, 8, 128)

    for pair in range(2):
        qs = [parts(4 * tb + 2 * pair + i, 0) for i in range(2)]

        def quad(uq, carry, diag):
            carry = list(carry)
            for ui in range(4):
                if diag and ui > 2 * pair + 1:
                    continue
                u = 4 * uq + ui
                k, v = parts(u, 1), parts(u, 2)
                for i in range(2):
                    if diag and ui > 2 * pair + i:
                        continue
                    e = jnp.exp2(POWER * jnp.tanh(jnp.sum(qs[i] * k, axis=0)))
                    carry[2 * i] = carry[2 * i] + e[None] * v
                    carry[2 * i + 1] = carry[2 * i + 1] + e
            return tuple(carry)

        zero = (jnp.zeros((8, 8, 128), jnp.float32), jnp.zeros((8, 128), jnp.float32)) * 2
        carry = lax.fori_loop(0, tb, lambda uq, c: quad(uq, c, False), zero)
        carry = quad(tb, carry, True)
        for i in range(2):
            a = carry[2 * i] * (1.0 / carry[2 * i + 1])[None]
            att[slot + 2 * pair + i] = a.reshape(64, 128)


def finish(blocks, att, mix, wout, gain, mlp_up, mlp_down):
    n = 4 * len(blocks)
    rows = jnp.concatenate([att[i].T for i in range(n)], axis=0).astype(jnp.bfloat16)
    o = dot(rows, wout[...])
    out = jnp.concatenate(
        [o[128 * i : 128 * i + 64, 0:128] + o[128 * i + 64 : 128 * i + 128, 128:256] for i in range(n)],
        axis=0,
    )
    m = jnp.concatenate([mix[pl.ds(4 * tb, 4)].reshape(256, 128) for tb in blocks], axis=0)
    stream = m.astype(jnp.float32) + out
    centre = jnp.mean(stream, axis=-1, keepdims=True)
    shifted = stream - centre
    spread = jnp.mean(shifted * shifted, axis=-1, keepdims=True)
    normed = (shifted * lax.rsqrt(spread + norm_eps) * gain[...]).astype(jnp.bfloat16)
    expanded = jnp.maximum(dot(normed, mlp_up[...]), 0.0).astype(jnp.bfloat16)
    done = (stream + dot(expanded, mlp_down[...])).astype(jnp.bfloat16)
    return done.reshape(len(blocks), 4, 64, 128)


def index_tables(z, x, cols, tab_v, slots_v):
    c = cols[...]
    lane = lax.broadcasted_iota(jnp.int32, (4, 4, 128), 2)
    tab = jnp.where(lane < 32, 3, 0)
    seen = []
    for k in range(8):
        ck = jnp.broadcast_to(c[:, :, k : k + 1], (4, 4, 128))
        blk = ck & 3
        dz = ((ck >> 4) - z) & 7
        dx = ((ck >> 2) - x) & 3
        pos = jnp.where(dz == 0, 0, jnp.where(dz <= 4, 2 * dz - 1, 16 - 2 * dz))
        ci = dx * 8 + pos
        seen.append((blk, ci))
        tab = jnp.where(
            ci == lane,
            jnp.minimum(tab, blk),
            jnp.where(ci + 32 == lane, jnp.maximum(tab, blk), tab),
        )
    low = jnp.min(tab, axis=1, keepdims=True)
    high = jnp.max(tab, axis=1, keepdims=True)
    tab = jnp.where(lane[:, 0:1] < 32, low, high)
    tab_v[...] = jnp.zeros((8, 128), jnp.int32)
    for s in range(4):
        tab_v[s : s + 1] = tab[s]
    slots = jnp.zeros((4, 4, 128), jnp.int32)
    for k, (blk, ci) in enumerate(seen):
        mine = jnp.sum(
            jnp.where(ci == lane, tab.astype(jnp.float32), 0.0), axis=2, keepdims=True
        )
        other = (blk.astype(jnp.float32) != mine).astype(jnp.int32)
        slots = jnp.where(lane == k, 2 * ci + other, slots)
    slots_v[...] = jnp.zeros((4, 8, 128), jnp.int32)
    slots_v[:, 0:4] = slots


class Sems:
    def __init__(self, send, recv):
        self.send, self.recv, self.n = send, recv, 0

    def copy(self, src, dst, device):
        i = self.n
        self.n += 1
        return pltpu.make_async_remote_copy(
            src, dst, self.send.at[i], self.recv.at[i], device_id=device, device_id_type=MESH
        )


COPIES = len(TABLE) + 4 * 8 + len(PAIRED) * (1 + 4 + 6) + 5 * (4 * 2 + len(DIRECT)) + 4 * 7 + 7


def kernel(
    feat_h, cols_h, tv_h, weight_h, positions_h, attn_proj_h, attn_out_h, gain_h, mlp_up_h,
    mlp_down_h, out,
    feat, cols, tv, weight, positions, attn_proj, attn_out, gain, mlp_up, mlp_down,
    tab_v, slots_v, tab_s, slots, tabr, tabs, picked, relay, stg_refs, hid, arr, wcat, wout, pos, mix, proj, att,
    obuf, oarr, send, recv, lsem, *bufs,
):
    bufs = list(bufs)
    comp = [bufs.pop(0) for _ in range(4)]
    own = [{dz: bufs.pop(0) for dz in range(1, 8)} for _ in range(4)]
    pair = {s: {dz: bufs.pop(0) for dz in (0, 1, 2, 6, 7)} for s in PAIRED}
    for s in range(4):
        own[s][0] = feat.at[s]
    kinds = {s: (1, 3) if s in PAIRED else (1, 3, 2) for s in range(4)}
    stg = {}
    for s in range(4):
        for k in kinds[s]:
            stg[s, k] = stg_refs.at[len(stg)]

    v = lax.axis_index("vert")
    t = lax.axis_index("tm")
    z, x = v // 4, v % 4
    near = {r: dict(vert=((z + r[0]) % 8) * 4 + (x + r[1]) % 4) for r in TABLE}
    up, down = near[1, 0], near[7, 0]
    side = {k: near[0, k] for k in (1, 2, 3)}
    times = {k: dict(tm=(t + k) % 8) for k in range(1, 8)}

    barrier = pltpu.get_barrier_semaphore()
    peers = list(near.values()) + list(times.values())
    for peer in peers:
        pl.semaphore_signal(barrier, inc=1, device_id=peer, device_id_type=MESH)

    loads = [
        pltpu.make_async_copy(src, dst, lsem.at[i])
        for i, (src, dst) in enumerate(
            [
                (cols_h, cols), (feat_h, feat), (attn_proj_h, attn_proj), (attn_out_h, attn_out),
                (positions_h, positions), (weight_h, weight), (gain_h, gain), (mlp_up_h, mlp_up),
                (mlp_down_h, mlp_down), (tv_h, tv),
            ]
        )
    ]
    for c in loads[:-1]:
        c.start()
    loads[0].wait()
    index_tables(z, x, cols, tab_v, slots_v)
    loads[1].wait()
    pl.semaphore_wait(barrier, len(peers))

    sems = Sems(send, recv)
    started = []

    def go(copy):
        copy.start()
        started.append(copy)
        return copy

    def ring(buf, step):
        if step < 4:
            a = sems.copy(buf[(9 - step) % 8], buf[8 - step], up)
            b = sems.copy(buf[step - 1], buf[step], down)
        else:
            a = sems.copy(buf[5].at[0:2], buf[4].at[0:2], up)
            b = sems.copy(buf[3].at[2:4], buf[4].at[2:4], down)
        return go(a), go(b)

    def place(dx, dz):
        return 2 * (dx * 8 + POS[dz])

    def narrow(s):
        passed = []
        for way, to, dz, first, second in ((0, up, 6, (1, 0), (2, 0)), (1, down, 2, (7, 0), (6, 0))):
            part = picked.at[PAIRED.index(s), way]
            far = 16 + POS[4] + 32 * way
            part[2] = pair[s][dz][tabs[TABLE[second], s, far]]
            end = 16 + POS[5 if way == 0 else 3]
            for w in range(2):
                part[w] = pair[s][dz][tabs[TABLE[first], s, 32 * w + end]]
        for way, to in ((0, up), (1, down)):
            part = picked.at[PAIRED.index(s), way]
            passed.append(go(sems.copy(part.at[2:3], relay.at[PAIRED.index(s), way], to)))
            q = place(2, 5 if way == 0 else 3)
            narrowed[s].append(go(sems.copy(part.at[0:2], comp[s].at[q : q + 2], to)))
        return passed

    def last(s):
        q = place(2, 4)
        for way, to in ((0, up), (1, down)):
            narrowed[s].append(
                go(
                    sems.copy(
                        relay.at[PAIRED.index(s), way], comp[s].at[q + way : q + way + 1], to
                    )
                )
            )

    narrowed = {s: [] for s in PAIRED}
    ringed = {}
    ringed[ORDER[0]] = ring(own[ORDER[0]], 1)
    tables = [
        go(sems.copy(tab_v, tabr.at[TABLE[(8 - r[0]) % 8, (4 - r[1]) % 4]], near[r]))
        for r in TABLE
    ]
    for s in ORDER[1:]:
        ringed[s] = ring(own[s], 1)
    swapped = {s: go(sems.copy(feat.at[s], pair[s][0], side[2])) for s in PAIRED}
    for c in loads[2:-1]:
        c.wait()
    mine = [
        pltpu.make_async_copy(tab_v, tab_s, lsem.at[0]),
        pltpu.make_async_copy(slots_v, slots, lsem.at[1]),
    ]
    for c in mine:
        c.start()
    arrange(attn_proj, attn_out, wcat, wout)
    pos[...] = positions[...].astype(jnp.float32).reshape(32, 1, 128)
    for c in mine:
        c.wait()
    for c in tables:
        c.wait_recv()
    theirs = [
        pltpu.make_async_copy(tabr.at[k], tabs.at[k], lsem.at[2 + k]) for k in range(len(TABLE))
    ]
    for c in theirs:
        c.start()
    for c in theirs:
        c.wait()

    loads[-1].start()
    crossed = {s: [] for s in range(4)}

    def keep(buf, s, dx, group):
        for dz in group:
            ci = dx * 8 + POS[dz]
            for w in range(2):
                comp[s][ci * 2 + w] = buf[dz][tab_s[s, w * 32 + ci]]

    def share(s, group):
        p0 = POS[group[0]]
        rows = 2 * len(group)
        for k in kinds[s]:
            for dz in group:
                for w in range(2):
                    ci = (4 - k) * 8 + POS[dz]
                    stg[s, k][POS[dz] * 2 + w] = own[s][dz][tabs[k - 1, s, w * 32 + ci]]
        keep(own[s], s, 0, group)
        for k in kinds[s]:
            q = (4 - k) * 16 + 2 * p0
            crossed[s].append(
                go(
                    sems.copy(
                        stg[s, k].at[2 * p0 : 2 * p0 + rows], comp[s].at[q : q + rows], side[k]
                    )
                )
            )

    sent = {}

    def spatial(s):
        for c in crossed[s] + narrowed.get(s, []):
            c.wait_recv()
        summed = []
        for r in range(4):
            left = jnp.concatenate([tv[s, r, k] for k in range(8)], axis=1)
            right = jnp.concatenate([comp[s][slots[s, r, k]] for k in range(8)], axis=0)
            summed.append(dot(left, right).astype(jnp.bfloat16))
        hidden = jnp.maximum(dot(jnp.concatenate(summed, axis=0), weight[...]), 0.0)
        hid[s] = hidden.astype(jnp.bfloat16).reshape(8, 64, 128)
        arr[t * 4 + s] = hid[s, t]
        sent[s] = [
            go(sems.copy(hid.at[s, (t + k) % 8], arr.at[t * 4 + s], times[k]))
            for k in range(1, 8)
        ]

    for s in ORDER:
        share(s, GROUPS[0])
    paired = {}

    def begin(s):
        swapped[s].wait_recv()
        paired[s] = ring(pair[s], 1)

    def advance(s, step):
        for c in paired[s]:
            c.wait_recv()
        if step == 1:
            paired[s] = ring(pair[s], 2)
            keep(pair[s], s, 2, GROUPS[0])
        elif step == 2:
            paired[s] = narrow(s)
        else:
            last(s)
        if step < 3:
            keep(pair[s], s, 2, GROUPS[step])

    for s in EARLY:
        begin(s)
    for step in range(1, 5):
        for s in ORDER:
            for c in ringed[s]:
                c.wait_recv()
            if step < 4:
                ringed[s] = ring(own[s], step + 1)
            share(s, GROUPS[step])
        for s in EARLY:
            if step < 4:
                advance(s, step)
        if step == 3:
            for s in LATE:
                begin(s)
    for step in range(1, 4):
        for s in LATE:
            advance(s, step)
    loads[-1].wait()
    for s in DIRECT + EARLY:
        spatial(s)
    for s in LATE:
        spatial(s)
    for s in DIRECT + EARLY + LATE:
        for c in sent[s]:
            c.wait_recv()
        for i in range(4):
            project(8 * i + s, 8 * i + 4 + s, arr, pos, wcat, mix, proj)

    def block(j):
        g = j // 2
        return (t // 2 + 2 + g + g // 2 + 2 * (g // 3)) % 4 * 2 + (t + j + g // 3) % 2

    def back(j):
        return pltpu.make_async_remote_copy(
            obuf.at[j], oarr.at[:, t], send.at[sems.n + j], recv.at[sems.n + j],
            device_id=dict(tm=block(j)), device_id_type=MESH,
        )

    @pl.loop(0, 3)
    def _(g):
        blocks = [block(2 * g + i) for i in range(2)]
        for i, tb in enumerate(blocks):
            attend(tb, proj, att, 4 * i)
        obuf[pl.ds(2 * g, 2)] = finish(blocks, att, mix, wout, gain, mlp_up, mlp_down)
        for i in range(2):
            back(2 * g + i).start()

    attend(block(6), proj, att)
    obuf[6:7] = finish([block(6)], att, mix, wout, gain, mlp_up, mlp_down)
    back(6).start()
    attend(t, proj, att)
    oarr[:, t] = finish([t], att, mix, wout, gain, mlp_up, mlp_down)[0]

    for c in started:
        c.wait_send()

    @pl.loop(0, 7)
    def _(j):
        back(j).wait_recv()

    out[...] = oarr[...]

    @pl.loop(0, 7)
    def _(j):
        back(j).wait_send()

    assert sems.n + 7 == COPIES


def local(
    features, tile_cols, tile_vals, space_weight, positions, attn_proj, attn_out, norm_gain,
    mlp_up, mlp_down,
):
    half, word, single = jnp.bfloat16, jnp.int32, jnp.float32
    block4 = pltpu.VMEM((4, 128, 128), half)
    embedded = pl.pallas_call(
        kernel,
        out_shape=jax.ShapeDtypeStruct((4, 8, 64, 128), half),
        in_specs=[pl.BlockSpec(memory_space=pltpu.HBM)] * 10,
        out_specs=pl.BlockSpec(memory_space=pltpu.VMEM),
        scratch_shapes=[
            pltpu.VMEM((4, 4, 128, 128), half),
            pltpu.VMEM((4, 4, 8), word),
            pltpu.VMEM((4, 4, 8, 128, 128), half),
            pltpu.VMEM((128, 128), half),
            pltpu.VMEM((32, 128), half),
            pltpu.VMEM((128, 384), half),
            pltpu.VMEM((128, 128), half),
            pltpu.VMEM((1, 128), single),
            pltpu.VMEM((128, 512), half),
            pltpu.VMEM((512, 128), half),
            pltpu.VMEM((8, 128), word),
            pltpu.VMEM((4, 8, 128), word),
            pltpu.SMEM((8, 128), word),
            pltpu.SMEM((4, 8, 128), word),
            pltpu.VMEM((len(TABLE), 8, 128), word),
            pltpu.SMEM((len(TABLE), 8, 128), word),
            pltpu.VMEM((len(PAIRED), 2, 3, 128, 128), half),
            pltpu.VMEM((len(PAIRED), 2, 1, 128, 128), half),
            pltpu.VMEM((2 * 4 + len(DIRECT), 16, 128, 128), half),
            pltpu.VMEM((4, 8, 64, 128), half),
            pltpu.VMEM((32, 64, 128), half),
            pltpu.VMEM((192, 256), half),
            pltpu.VMEM((64, 256), half),
            pltpu.VMEM((32, 1, 128), single),
            pltpu.VMEM((32, 64, 128), half),
            pltpu.VMEM((32, 192, 128), single),
            pltpu.VMEM((8, 64, 128), single),
            pltpu.VMEM((7, 4, 64, 128), half),
            pltpu.VMEM((4, 8, 64, 128), half),
            pltpu.SemaphoreType.DMA((COPIES,)),
            pltpu.SemaphoreType.DMA((COPIES,)),
            pltpu.SemaphoreType.DMA((10,)),
        ]
        + [pltpu.VMEM((64, 128, 128), half)] * 4
        + [block4] * 28
        + [block4] * (5 * len(PAIRED)),
        compiler_params=pltpu.CompilerParams(
            collective_id=0, has_side_effects=True, vmem_limit_bytes=44 * 2**20
        ),
    )(
        *[
            pltpu.with_memory_space_constraint(a, pltpu.HBM)
            for a in (
                features.reshape(4, 4, 128, 128), tile_cols, tile_vals, space_weight, positions,
                attn_proj, attn_out, norm_gain.reshape(1, 128), mlp_up, mlp_down,
            )
        ]
    )
    return embedded.reshape(4, 512, 128)


def solution(mesh):
    placed = (
        P("tm", "vert", None),
        P("tm", "vert", None),
        P("tm", "vert", None, None, None),
        P(),
        P(),
        P(),
        P(),
        P(),
        P(),
        P(),
    )
    return jax.shard_map(
        local, mesh=mesh, in_specs=placed, out_specs=P("tm", "vert", None), check_vma=False
    )
```

```python
import math

import jax
import jax.numpy as jnp
from jax import lax
from jax.experimental import pallas as pl
from jax.experimental.pallas import tpu as pltpu
from jax.sharding import PartitionSpec as P

MESH = pl.DeviceIdType.MESH
norm_eps = 1e-05
SCORE = 1.0 / (4.0 * math.sqrt(8.0))
POWER = 4.0 * math.log2(math.e)

ZORD = (0, 1, 7, 2, 6, 3, 5, 4)
POS = {dz: p for p, dz in enumerate(ZORD)}
GROUPS = ((0,), (1, 7), (2, 6), (3, 5), (4,))
PAIRED = (0, 1, 2)
DIRECT = (3,)
EARLY, LATE = (0,), (1, 2)
ORDER = (3, 0, 1, 2)
TABLE = {(0, 1): 0, (0, 2): 1, (0, 3): 2, (1, 0): 3, (2, 0): 4, (7, 0): 5, (6, 0): 6}


def dot_t(a, b):
    return lax.dot_general(a, b, (((1,), (1,)), ((), ())), preferred_element_type=jnp.float32)


def dot(a, b):
    return jnp.dot(a, b, preferred_element_type=jnp.float32)


def arrange(attn_proj, attn_out, wcat, wout):
    row = lax.broadcasted_iota(jnp.int32, (192, 384), 0)
    col = lax.broadcasted_iota(jnp.int32, (192, 384), 1)
    base = (row // 64) * 128 + (row % 8) * 8 + (row // 8) % 8
    for half in range(2):
        pick = (col == base + half * 64).astype(jnp.bfloat16)
        wcat[:, half * 128 : (half + 1) * 128] = dot_t(pick, attn_proj[...]).astype(jnp.bfloat16)
    row = lax.broadcasted_iota(jnp.int32, (64, 128), 0)
    col = lax.broadcasted_iota(jnp.int32, (64, 128), 1)
    base = (row % 8) * 8 + row // 8
    for half in range(2):
        pick = (col == base + half * 64).astype(jnp.bfloat16)
        wout[:, half * 128 : (half + 1) * 128] = dot(pick, attn_out[...]).astype(jnp.bfloat16)


def project(t0, t1, arr, pos, wcat, mix, proj):
    zero = jnp.zeros((64, 128), jnp.bfloat16)
    rows = []
    for t in (t0, t1):
        m = (arr[t].astype(jnp.float32) + pos[t]).astype(jnp.bfloat16)
        mix[t] = m
        rows.append(jnp.concatenate([m, zero], axis=1))
        rows.append(jnp.concatenate([zero, m], axis=1))
    both = jnp.concatenate(rows, axis=0)
    p = dot_t(wcat[...], both).astype(jnp.bfloat16).astype(jnp.float32)
    for i, t in enumerate((t0, t1)):
        q = p[:, i * 128 : (i + 1) * 128]
        proj[t, 0:64] = q[0:64] * SCORE
        proj[t, 64:192] = q[64:192]


def attend(tb, proj, att, slot=0):
    def parts(t, k):
        return proj[t, 64 * k : 64 * (k + 1)].reshape(8, 8, 128)

    for pair in range(2):
        qs = [parts(4 * tb + 2 * pair + i, 0) for i in range(2)]

        def quad(uq, carry, diag):
            carry = list(carry)
            for ui in range(4):
                if diag and ui > 2 * pair + 1:
                    continue
                u = 4 * uq + ui
                k, v = parts(u, 1), parts(u, 2)
                for i in range(2):
                    if diag and ui > 2 * pair + i:
                        continue
                    e = jnp.exp2(POWER * jnp.tanh(jnp.sum(qs[i] * k, axis=0)))
                    carry[2 * i] = carry[2 * i] + e[None] * v
                    carry[2 * i + 1] = carry[2 * i + 1] + e
            return tuple(carry)

        zero = (jnp.zeros((8, 8, 128), jnp.float32), jnp.zeros((8, 128), jnp.float32)) * 2
        carry = lax.fori_loop(0, tb, lambda uq, c: quad(uq, c, False), zero)
        carry = quad(tb, carry, True)
        for i in range(2):
            a = carry[2 * i] * (1.0 / carry[2 * i + 1])[None]
            att[slot + 2 * pair + i] = a.reshape(64, 128)


def finish(blocks, att, mix, wout, gain, mlp_up, mlp_down):
    n = 4 * len(blocks)
    rows = jnp.concatenate([att[i].T for i in range(n)], axis=0).astype(jnp.bfloat16)
    o = dot(rows, wout[...])
    out = jnp.concatenate(
        [o[128 * i : 128 * i + 64, 0:128] + o[128 * i + 64 : 128 * i + 128, 128:256] for i in range(n)],
        axis=0,
    )
    m = jnp.concatenate([mix[pl.ds(4 * tb, 4)].reshape(256, 128) for tb in blocks], axis=0)
    stream = m.astype(jnp.float32) + out
    centre = jnp.mean(stream, axis=-1, keepdims=True)
    shifted = stream - centre
    spread = jnp.mean(shifted * shifted, axis=-1, keepdims=True)
    normed = (shifted * lax.rsqrt(spread + norm_eps) * gain[...]).astype(jnp.bfloat16)
    expanded = jnp.maximum(dot(normed, mlp_up[...]), 0.0).astype(jnp.bfloat16)
    done = (stream + dot(expanded, mlp_down[...])).astype(jnp.bfloat16)
    return done.reshape(len(blocks), 4, 64, 128)


def index_tables(z, x, cols, tab_v, slots_v):
    c = cols[...]
    lane = lax.broadcasted_iota(jnp.int32, (4, 4, 128), 2)
    tab = jnp.where(lane < 32, 3, 0)
    seen = []
    for k in range(8):
        ck = jnp.broadcast_to(c[:, :, k : k + 1], (4, 4, 128))
        blk = ck & 3
        dz = ((ck >> 4) - z) & 7
        dx = ((ck >> 2) - x) & 3
        pos = jnp.where(dz == 0, 0, jnp.where(dz <= 4, 2 * dz - 1, 16 - 2 * dz))
        ci = dx * 8 + pos
        seen.append((blk, ci))
        tab = jnp.where(
            ci == lane,
            jnp.minimum(tab, blk),
            jnp.where(ci + 32 == lane, jnp.maximum(tab, blk), tab),
        )
    low = jnp.min(tab, axis=1, keepdims=True)
    high = jnp.max(tab, axis=1, keepdims=True)
    tab = jnp.where(lane[:, 0:1] < 32, low, high)
    tab_v[...] = jnp.zeros((8, 128), jnp.int32)
    for s in range(4):
        tab_v[s : s + 1] = tab[s]
    slots = jnp.zeros((4, 4, 128), jnp.int32)
    for k, (blk, ci) in enumerate(seen):
        mine = jnp.sum(
            jnp.where(ci == lane, tab.astype(jnp.float32), 0.0), axis=2, keepdims=True
        )
        other = (blk.astype(jnp.float32) != mine).astype(jnp.int32)
        slots = jnp.where(lane == k, 2 * ci + other, slots)
    slots_v[...] = jnp.zeros((4, 8, 128), jnp.int32)
    slots_v[:, 0:4] = slots


class Sems:
    def __init__(self, send, recv):
        self.send, self.recv, self.n = send, recv, 0

    def copy(self, src, dst, device):
        i = self.n
        self.n += 1
        return pltpu.make_async_remote_copy(
            src, dst, self.send.at[i], self.recv.at[i], device_id=device, device_id_type=MESH
        )


COPIES = len(TABLE) + 4 * 8 + len(PAIRED) * (1 + 4 + 4) + 5 * (4 * 2 + len(DIRECT)) + 4 * 7 + 7


def kernel(
    feat_h, cols_h, tv_h, weight_h, positions_h, attn_proj_h, attn_out_h, gain_h, mlp_up_h,
    mlp_down_h, out,
    feat, cols, tv, weight, positions, attn_proj, attn_out, gain, mlp_up, mlp_down,
    tab_v, slots_v, tab_s, slots, tabr, tabs, picked, stg_refs, hid, arr, wcat, wout, pos, mix, proj, att,
    obuf, oarr, send, recv, lsem, *bufs,
):
    bufs = list(bufs)
    comp = [bufs.pop(0) for _ in range(4)]
    own = [{dz: bufs.pop(0) for dz in range(1, 8)} for _ in range(4)]
    pair = {s: {dz: bufs.pop(0) for dz in (0, 1, 2, 6, 7)} for s in PAIRED}
    for s in range(4):
        own[s][0] = feat.at[s]
    kinds = {s: (1, 3) if s in PAIRED else (1, 3, 2) for s in range(4)}
    stg = {}
    for s in range(4):
        for k in kinds[s]:
            stg[s, k] = stg_refs.at[len(stg)]

    v = lax.axis_index("vert")
    t = lax.axis_index("tm")
    z, x = v // 4, v % 4
    near = {r: dict(vert=((z + r[0]) % 8) * 4 + (x + r[1]) % 4) for r in TABLE}
    up, down = near[1, 0], near[7, 0]
    side = {k: near[0, k] for k in (1, 2, 3)}
    times = {k: dict(tm=(t + k) % 8) for k in range(1, 8)}

    barrier = pltpu.get_barrier_semaphore()
    peers = list(near.values()) + list(times.values())
    for peer in peers:
        pl.semaphore_signal(barrier, inc=1, device_id=peer, device_id_type=MESH)

    loads = [
        pltpu.make_async_copy(src, dst, lsem.at[i])
        for i, (src, dst) in enumerate(
            [
                (cols_h, cols), (feat_h, feat), (attn_proj_h, attn_proj), (attn_out_h, attn_out),
                (positions_h, positions), (weight_h, weight), (gain_h, gain), (mlp_up_h, mlp_up),
                (mlp_down_h, mlp_down), (tv_h, tv),
            ]
        )
    ]
    for c in loads[:-1]:
        c.start()
    loads[1].wait()
    pl.semaphore_wait(barrier, len(peers))

    sems = Sems(send, recv)
    started = []

    def go(copy):
        copy.start()
        started.append(copy)
        return copy

    def ring(buf, step):
        if step < 4:
            a = sems.copy(buf[(9 - step) % 8], buf[8 - step], up)
            b = sems.copy(buf[step - 1], buf[step], down)
        else:
            a = sems.copy(buf[5].at[0:2], buf[4].at[0:2], up)
            b = sems.copy(buf[3].at[2:4], buf[4].at[2:4], down)
        return go(a), go(b)

    def place(dx, dz):
        return 2 * (dx * 8 + POS[dz])

    def narrow(s):
        ends = ((6, (1, 0), (2, 0), 5), (2, (7, 0), (6, 0), 3))
        for way, (dz, first, second, end) in enumerate(ends):
            part = picked.at[PAIRED.index(s), way]
            part[2] = pair[s][dz][tabs[TABLE[second], s, 32 * way + 16 + POS[4]]]
            for w in range(2):
                part[w] = pair[s][dz][tabs[TABLE[first], s, 32 * w + 16 + POS[end]]]
        for way, (dz, first, second, end) in enumerate(ends):
            part = picked.at[PAIRED.index(s), way]
            q = place(2, 4) + way
            narrowed[s].append(
                go(sems.copy(part.at[2:3], comp[s].at[q : q + 1], near[second]))
            )
            q = place(2, end)
            narrowed[s].append(go(sems.copy(part.at[0:2], comp[s].at[q : q + 2], near[first])))

    narrowed = {s: [] for s in PAIRED}
    ringed = {ORDER[0]: ring(own[ORDER[0]], 1)}
    loads[0].wait()
    index_tables(z, x, cols, tab_v, slots_v)

    def tell(r):
        return go(sems.copy(tab_v, tabr.at[TABLE[(8 - r[0]) % 8, (4 - r[1]) % 4]], near[r]))

    def hear(tables, held):
        for c in tables:
            c.wait_recv()
        held = [pltpu.make_async_copy(tabr.at[k], tabs.at[k], lsem.at[2 + k]) for k in held]
        for c in held:
            c.start()
        for c in held:
            c.wait()

    sideways = [tell(r) for r in TABLE if r[1]]
    swapped = {s: go(sems.copy(feat.at[s], pair[s][0], side[2])) for s in PAIRED}
    for s in ORDER[1:]:
        ringed[s] = ring(own[s], 1)
    along = [tell(r) for r in TABLE if r[0]]
    mine = [
        pltpu.make_async_copy(tab_v, tab_s, lsem.at[0]),
        pltpu.make_async_copy(slots_v, slots, lsem.at[1]),
    ]
    for c in loads[2:-1]:
        c.wait()
    for c in mine:
        c.start()
    arrange(attn_proj, attn_out, wcat, wout)
    pos[...] = positions[...].astype(jnp.float32).reshape(32, 1, 128)
    for c in mine:
        c.wait()
    hear(sideways, range(3))
    loads[-1].start()
    crossed = {s: [] for s in range(4)}

    def keep(buf, s, dx, group):
        for dz in group:
            ci = dx * 8 + POS[dz]
            for w in range(2):
                comp[s][ci * 2 + w] = buf[dz][tab_s[s, w * 32 + ci]]

    def share(s, group):
        p0 = POS[group[0]]
        rows = 2 * len(group)
        for k in kinds[s]:
            for dz in group:
                for w in range(2):
                    ci = (4 - k) * 8 + POS[dz]
                    stg[s, k][POS[dz] * 2 + w] = own[s][dz][tabs[k - 1, s, w * 32 + ci]]
        keep(own[s], s, 0, group)
        for k in kinds[s]:
            q = (4 - k) * 16 + 2 * p0
            crossed[s].append(
                go(
                    sems.copy(
                        stg[s, k].at[2 * p0 : 2 * p0 + rows], comp[s].at[q : q + rows], side[k]
                    )
                )
            )

    sent = {}

    def spatial(s):
        for c in crossed[s] + narrowed.get(s, []):
            c.wait_recv()
        summed = []
        far = [(t // 2 + k) % 4 for k in (2, 1, 3, 0)]
        for r in far:
            left = jnp.concatenate([tv[s, r, k] for k in range(8)], axis=1)
            right = jnp.concatenate([comp[s][slots[s, r, k]] for k in range(8)], axis=0)
            summed.append(dot(left, right).astype(jnp.bfloat16))
        for i in range(4):
            hidden = jnp.maximum(dot(summed[i], weight[...]), 0.0).astype(jnp.bfloat16)
            hid[s, pl.ds(2 * far[i], 2)] = hidden.reshape(2, 64, 128)
        arr[t * 4 + s] = hid[s, t]
        sent[s] = []
        for i, k in enumerate((2, 1, 3, 0)):
            for core in range(2):
                if k or core:
                    peer = far[i] * 2 + (t + core) % 2
                    sent[s].append(
                        go(sems.copy(hid.at[s, peer], arr.at[t * 4 + s], dict(tm=peer)))
                    )

    for s in ORDER:
        share(s, GROUPS[0])
    paired = {}

    def begin(s):
        swapped[s].wait_recv()
        paired[s] = ring(pair[s], 1)

    def advance(s, step):
        for c in paired[s]:
            c.wait_recv()
        if step == 1:
            paired[s] = ring(pair[s], 2)
            keep(pair[s], s, 2, GROUPS[0])
        else:
            narrow(s)
        keep(pair[s], s, 2, GROUPS[step])

    for s in EARLY:
        begin(s)
    for step in range(1, 5):
        for s in ORDER:
            for c in ringed[s]:
                c.wait_recv()
            if step < 4:
                ringed[s] = ring(own[s], step + 1)
            share(s, GROUPS[step])
        for s in EARLY:
            if step < 3:
                advance(s, step)
        if step == 1:
            hear(along, range(3, 7))
        if step == 3:
            for s in LATE:
                begin(s)
    for step in range(1, 3):
        for s in LATE:
            advance(s, step)
    loads[-1].wait()
    for s in DIRECT + EARLY:
        spatial(s)
    for s in LATE:
        spatial(s)
    for s in DIRECT + EARLY + LATE[:1]:
        for c in sent[s]:
            c.wait_recv()

    @pl.loop(0, 4)
    def _(i):
        s = (3 + i) % 4

        @pl.when(i == 3)
        def _():
            for c in sent[2]:
                c.wait_recv()

        for k in range(4):
            project(8 * k + s, 8 * k + 4 + s, arr, pos, wcat, mix, proj)

    def block(j):
        g = j // 2
        return (t // 2 + 2 + g + g // 2 + 2 * (g // 3)) % 4 * 2 + (t + j + g // 3) % 2

    def back(j):
        return pltpu.make_async_remote_copy(
            obuf.at[j], oarr.at[:, t], send.at[sems.n + j], recv.at[sems.n + j],
            device_id=dict(tm=block(j)), device_id_type=MESH,
        )

    @pl.loop(0, 3)
    def _(g):
        blocks = [block(2 * g + i) for i in range(2)]
        for i, tb in enumerate(blocks):
            attend(tb, proj, att, 4 * i)
        obuf[pl.ds(2 * g, 2)] = finish(blocks, att, mix, wout, gain, mlp_up, mlp_down)
        for i in range(2):
            back(2 * g + i).start()

    @pl.loop(6, 8)
    def _(j):
        attend(block(j), proj, att)
        obuf[pl.ds(j, 1)] = finish([block(j)], att, mix, wout, gain, mlp_up, mlp_down)

        @pl.when(j == 6)
        def _():
            back(6).start()

    oarr[:, t] = obuf[7]

    for c in started:
        c.wait_send()

    @pl.loop(0, 7)
    def _(j):
        back(j).wait_recv()

    out[...] = oarr[...]

    @pl.loop(0, 7)
    def _(j):
        back(j).wait_send()

    assert sems.n + 7 == COPIES


def local(
    features, tile_cols, tile_vals, space_weight, positions, attn_proj, attn_out, norm_gain,
    mlp_up, mlp_down,
):
    half, word, single = jnp.bfloat16, jnp.int32, jnp.float32
    block4 = pltpu.VMEM((4, 128, 128), half)
    embedded = pl.pallas_call(
        kernel,
        out_shape=jax.ShapeDtypeStruct((4, 8, 64, 128), half),
        in_specs=[pl.BlockSpec(memory_space=pltpu.HBM)] * 10,
        out_specs=pl.BlockSpec(memory_space=pltpu.VMEM),
        scratch_shapes=[
            pltpu.VMEM((4, 4, 128, 128), half),
            pltpu.VMEM((4, 4, 8), word),
            pltpu.VMEM((4, 4, 8, 128, 128), half),
            pltpu.VMEM((128, 128), half),
            pltpu.VMEM((32, 128), half),
            pltpu.VMEM((128, 384), half),
            pltpu.VMEM((128, 128), half),
            pltpu.VMEM((1, 128), single),
            pltpu.VMEM((128, 512), half),
            pltpu.VMEM((512, 128), half),
            pltpu.VMEM((8, 128), word),
            pltpu.VMEM((4, 8, 128), word),
            pltpu.SMEM((8, 128), word),
            pltpu.SMEM((4, 8, 128), word),
            pltpu.VMEM((len(TABLE), 8, 128), word),
            pltpu.SMEM((len(TABLE), 8, 128), word),
            pltpu.VMEM((len(PAIRED), 2, 3, 128, 128), half),
            pltpu.VMEM((2 * 4 + len(DIRECT), 16, 128, 128), half),
            pltpu.VMEM((4, 8, 64, 128), half),
            pltpu.VMEM((32, 64, 128), half),
            pltpu.VMEM((192, 256), half),
            pltpu.VMEM((64, 256), half),
            pltpu.VMEM((32, 1, 128), single),
            pltpu.VMEM((32, 64, 128), half),
            pltpu.VMEM((32, 192, 128), single),
            pltpu.VMEM((16, 64, 128), single),
            pltpu.VMEM((8, 4, 64, 128), half),
            pltpu.VMEM((4, 8, 64, 128), half),
            pltpu.SemaphoreType.DMA((COPIES,)),
            pltpu.SemaphoreType.DMA((COPIES,)),
            pltpu.SemaphoreType.DMA((10,)),
        ]
        + [pltpu.VMEM((64, 128, 128), half)] * 4
        + [block4] * 28
        + [block4] * (5 * len(PAIRED)),
        compiler_params=pltpu.CompilerParams(
            collective_id=0, has_side_effects=True, vmem_limit_bytes=44 * 2**20
        ),
    )(
        *[
            pltpu.with_memory_space_constraint(a, pltpu.HBM)
            for a in (
                features.reshape(4, 4, 128, 128), tile_cols, tile_vals, space_weight, positions,
                attn_proj, attn_out, norm_gain.reshape(1, 128), mlp_up, mlp_down,
            )
        ]
    )
    return embedded.reshape(4, 512, 128)


def solution(mesh):
    placed = (
        P("tm", "vert", None),
        P("tm", "vert", None),
        P("tm", "vert", None, None, None),
        P(),
        P(),
        P(),
        P(),
        P(),
        P(),
        P(),
    )
    return jax.shard_map(
        local, mesh=mesh, in_specs=placed, out_specs=P("tm", "vert", None), check_vma=False
    )
```

```python
import math

import jax
import jax.numpy as jnp
from jax import lax
from jax.experimental import pallas as pl
from jax.experimental.pallas import tpu as pltpu
from jax.sharding import PartitionSpec as P

MESH = pl.DeviceIdType.MESH
norm_eps = 1e-05
SCORE = 1.0 / (4.0 * math.sqrt(8.0))
POWER = 4.0 * math.log2(math.e)

ZORD = (0, 1, 7, 2, 6, 3, 5, 4)
POS = {dz: p for p, dz in enumerate(ZORD)}
GROUPS = ((0,), (1, 7), (2, 6), (3, 5), (4,))
PAIRED = (0, 1, 2)
DIRECT = (3,)
EARLY, LATE = (0,), (1, 2)
ORDER = (3, 0, 1, 2)
TABLE = {(0, 1): 0, (0, 2): 1, (0, 3): 2, (1, 0): 3, (2, 0): 4, (7, 0): 5, (6, 0): 6}


def dot_t(a, b):
    return lax.dot_general(a, b, (((1,), (1,)), ((), ())), preferred_element_type=jnp.float32)


def dot(a, b):
    return jnp.dot(a, b, preferred_element_type=jnp.float32)


def arrange(attn_proj, attn_out, wcat, wout):
    row = lax.broadcasted_iota(jnp.int32, (192, 384), 0)
    col = lax.broadcasted_iota(jnp.int32, (192, 384), 1)
    base = (row // 64) * 128 + (row % 8) * 8 + (row // 8) % 8
    for half in range(2):
        pick = (col == base + half * 64).astype(jnp.bfloat16)
        wcat[:, half * 128 : (half + 1) * 128] = dot_t(pick, attn_proj[...]).astype(jnp.bfloat16)
    row = lax.broadcasted_iota(jnp.int32, (64, 128), 0)
    col = lax.broadcasted_iota(jnp.int32, (64, 128), 1)
    base = (row % 8) * 8 + row // 8
    for half in range(2):
        pick = (col == base + half * 64).astype(jnp.bfloat16)
        wout[:, half * 128 : (half + 1) * 128] = dot(pick, attn_out[...]).astype(jnp.bfloat16)


def project(t0, t1, arr, pos, wcat, mix, proj):
    zero = jnp.zeros((64, 128), jnp.bfloat16)
    rows = []
    for t in (t0, t1):
        m = (arr[t].astype(jnp.float32) + pos[t]).astype(jnp.bfloat16)
        mix[t] = m
        rows.append(jnp.concatenate([m, zero], axis=1))
        rows.append(jnp.concatenate([zero, m], axis=1))
    both = jnp.concatenate(rows, axis=0)
    p = dot_t(wcat[...], both).astype(jnp.bfloat16).astype(jnp.float32)
    for i, t in enumerate((t0, t1)):
        q = p[:, i * 128 : (i + 1) * 128]
        proj[t, 0:64] = q[0:64] * SCORE
        proj[t, 64:192] = q[64:192]


def attend(tb, proj, att, slot=0):
    def parts(t, k):
        return proj[t, 64 * k : 64 * (k + 1)].reshape(8, 8, 128)

    for pair in range(2):
        qs = [parts(4 * tb + 2 * pair + i, 0) for i in range(2)]

        def quad(uq, carry, diag):
            carry = list(carry)
            for ui in range(4):
                if diag and ui > 2 * pair + 1:
                    continue
                u = 4 * uq + ui
                k, v = parts(u, 1), parts(u, 2)
                for i in range(2):
                    if diag and ui > 2 * pair + i:
                        continue
                    e = jnp.exp2(POWER * jnp.tanh(jnp.sum(qs[i] * k, axis=0)))
                    carry[2 * i] = carry[2 * i] + e[None] * v
                    carry[2 * i + 1] = carry[2 * i + 1] + e
            return tuple(carry)

        zero = (jnp.zeros((8, 8, 128), jnp.float32), jnp.zeros((8, 128), jnp.float32)) * 2
        carry = lax.fori_loop(0, tb, lambda uq, c: quad(uq, c, False), zero)
        carry = quad(tb, carry, True)
        for i in range(2):
            a = carry[2 * i] * (1.0 / carry[2 * i + 1])[None]
            att[slot + 2 * pair + i] = a.reshape(64, 128)


def finish(blocks, att, mix, wout, gain, mlp_up, mlp_down):
    n = 4 * len(blocks)
    out = []
    for i in range(n):
        o = lax.dot_general(
            att[i].astype(jnp.bfloat16), wout[...], (((0,), (0,)), ((), ())),
            preferred_element_type=jnp.float32,
        )
        out.append(o[0:64, 0:128] + o[64:128, 128:256])
    out = jnp.concatenate(out, axis=0)
    m = jnp.concatenate([mix[pl.ds(4 * tb, 4)].reshape(256, 128) for tb in blocks], axis=0)
    stream = m.astype(jnp.float32) + out
    centre = jnp.mean(stream, axis=-1, keepdims=True)
    shifted = stream - centre
    spread = jnp.mean(shifted * shifted, axis=-1, keepdims=True)
    normed = (shifted * lax.rsqrt(spread + norm_eps) * gain[...]).astype(jnp.bfloat16)
    expanded = jnp.maximum(dot(normed, mlp_up[...]), 0.0).astype(jnp.bfloat16)
    done = (stream + dot(expanded, mlp_down[...])).astype(jnp.bfloat16)
    return done.reshape(len(blocks), 4, 64, 128)


def index_tables(z, x, cols, tab_v, slots_v):
    c = cols[...]
    lane = lax.broadcasted_iota(jnp.int32, (4, 4, 128), 2)
    tab = jnp.where(lane < 32, 3, 0)
    seen = []
    for k in range(8):
        ck = jnp.broadcast_to(c[:, :, k : k + 1], (4, 4, 128))
        blk = ck & 3
        dz = ((ck >> 4) - z) & 7
        dx = ((ck >> 2) - x) & 3
        pos = jnp.where(dz == 0, 0, jnp.where(dz <= 4, 2 * dz - 1, 16 - 2 * dz))
        ci = dx * 8 + pos
        seen.append((blk, ci))
        tab = jnp.where(
            ci == lane,
            jnp.minimum(tab, blk),
            jnp.where(ci + 32 == lane, jnp.maximum(tab, blk), tab),
        )
    low = jnp.min(tab, axis=1, keepdims=True)
    high = jnp.max(tab, axis=1, keepdims=True)
    tab = jnp.where(lane[:, 0:1] < 32, low, high)
    tab_v[...] = jnp.zeros((8, 128), jnp.int32)
    for s in range(4):
        tab_v[s : s + 1] = tab[s]
    slots = jnp.zeros((4, 4, 128), jnp.int32)
    for k, (blk, ci) in enumerate(seen):
        mine = jnp.sum(
            jnp.where(ci == lane, tab.astype(jnp.float32), 0.0), axis=2, keepdims=True
        )
        other = (blk.astype(jnp.float32) != mine).astype(jnp.int32)
        slots = jnp.where(lane == k, 2 * ci + other, slots)
    slots_v[...] = jnp.zeros((4, 8, 128), jnp.int32)
    slots_v[:, 0:4] = slots


class Sems:
    def __init__(self, send, recv):
        self.send, self.recv, self.n = send, recv, 0

    def copy(self, src, dst, device):
        i = self.n
        self.n += 1
        return pltpu.make_async_remote_copy(
            src, dst, self.send.at[i], self.recv.at[i], device_id=device, device_id_type=MESH
        )


COPIES = len(TABLE) + 4 * 8 + len(PAIRED) * (1 + 4 + 4) + 5 * (4 * 2 + len(DIRECT)) + 4 * 7 + 7


def kernel(
    feat_h, cols_h, tv_h, weight_h, positions_h, attn_proj_h, attn_out_h, gain_h, mlp_up_h,
    mlp_down_h, out,
    feat, cols, tv, weight, positions, attn_proj, attn_out, gain, mlp_up, mlp_down,
    tab_v, slots_v, tab_s, slots, tabr, tabs, picked, stg_refs, hid, arr, wcat, wout, pos, mix, proj, att,
    obuf, oarr, send, recv, lsem, *bufs,
):
    bufs = list(bufs)
    comp = [bufs.pop(0) for _ in range(4)]
    own = [{dz: bufs.pop(0) for dz in range(1, 8)} for _ in range(4)]
    pair = {s: {dz: bufs.pop(0) for dz in (0, 1, 2, 6, 7)} for s in PAIRED}
    for s in range(4):
        own[s][0] = feat.at[s]
    kinds = {s: (1, 3) if s in PAIRED else (1, 3, 2) for s in range(4)}
    stg = {}
    for s in range(4):
        for k in kinds[s]:
            stg[s, k] = stg_refs.at[len(stg)]

    v = lax.axis_index("vert")
    t = lax.axis_index("tm")
    z, x = v // 4, v % 4
    near = {r: dict(vert=((z + r[0]) % 8) * 4 + (x + r[1]) % 4) for r in TABLE}
    up, down = near[1, 0], near[7, 0]
    side = {k: near[0, k] for k in (1, 2, 3)}
    times = {k: dict(tm=(t + k) % 8) for k in range(1, 8)}

    barrier = pltpu.get_barrier_semaphore()
    peers = list(near.values()) + list(times.values())
    for peer in peers:
        pl.semaphore_signal(barrier, inc=1, device_id=peer, device_id_type=MESH)

    loads = [
        pltpu.make_async_copy(src, dst, lsem.at[i])
        for i, (src, dst) in enumerate(
            [
                (cols_h, cols), (feat_h, feat), (attn_proj_h, attn_proj), (attn_out_h, attn_out),
                (positions_h, positions), (weight_h, weight), (gain_h, gain), (mlp_up_h, mlp_up),
                (mlp_down_h, mlp_down), (tv_h, tv),
            ]
        )
    ]
    for c in loads[:-1]:
        c.start()
    loads[1].wait()
    pl.semaphore_wait(barrier, len(peers))

    sems = Sems(send, recv)
    started = []

    def go(copy):
        copy.start()
        started.append(copy)
        return copy

    def ring(buf, step):
        if step < 4:
            a = sems.copy(buf[(9 - step) % 8], buf[8 - step], up)
            b = sems.copy(buf[step - 1], buf[step], down)
        else:
            a = sems.copy(buf[5].at[0:2], buf[4].at[0:2], up)
            b = sems.copy(buf[3].at[2:4], buf[4].at[2:4], down)
        return go(a), go(b)

    def place(dx, dz):
        return 2 * (dx * 8 + POS[dz])

    def narrow(s):
        ends = ((6, (1, 0), (2, 0), 5), (2, (7, 0), (6, 0), 3))
        for way, (dz, first, second, end) in enumerate(ends):
            part = picked.at[PAIRED.index(s), way]
            part[2] = pair[s][dz][tabs[TABLE[second], s, 32 * way + 16 + POS[4]]]
            for w in range(2):
                part[w] = pair[s][dz][tabs[TABLE[first], s, 32 * w + 16 + POS[end]]]
        for way, (dz, first, second, end) in enumerate(ends):
            part = picked.at[PAIRED.index(s), way]
            q = place(2, 4) + way
            narrowed[s].append(
                go(sems.copy(part.at[2:3], comp[s].at[q : q + 1], near[second]))
            )
            q = place(2, end)
            narrowed[s].append(go(sems.copy(part.at[0:2], comp[s].at[q : q + 2], near[first])))

    narrowed = {s: [] for s in PAIRED}
    ringed = {ORDER[0]: ring(own[ORDER[0]], 1)}

    def swap(s):
        return go(sems.copy(feat.at[s], pair[s][0], side[2]))

    swapped = {PAIRED[0]: swap(PAIRED[0])}
    loads[0].wait()
    index_tables(z, x, cols, tab_v, slots_v)

    def tell(r):
        return go(sems.copy(tab_v, tabr.at[TABLE[(8 - r[0]) % 8, (4 - r[1]) % 4]], near[r]))

    def hear(tables, held):
        for c in tables:
            c.wait_recv()
        held = [pltpu.make_async_copy(tabr.at[k], tabs.at[k], lsem.at[2 + k]) for k in held]
        for c in held:
            c.start()
        for c in held:
            c.wait()

    sideways = [tell(r) for r in TABLE if r[1]]
    swapped |= {s: swap(s) for s in PAIRED[1:]}
    for s in ORDER[1:]:
        ringed[s] = ring(own[s], 1)
    along = [tell(r) for r in TABLE if r[0]]
    mine = [
        pltpu.make_async_copy(tab_v, tab_s, lsem.at[0]),
        pltpu.make_async_copy(slots_v, slots, lsem.at[1]),
    ]
    for c in loads[2:-1]:
        c.wait()
    for c in mine:
        c.start()
    arrange(attn_proj, attn_out, wcat, wout)
    pos[...] = positions[...].astype(jnp.float32).reshape(32, 1, 128)
    for c in mine:
        c.wait()
    hear(sideways, range(3))
    loads[-1].start()
    crossed = {s: [] for s in range(4)}

    def keep(buf, s, dx, group):
        for dz in group:
            ci = dx * 8 + POS[dz]
            for w in range(2):
                comp[s][ci * 2 + w] = buf[dz][tab_s[s, w * 32 + ci]]

    def share(s, group):
        p0 = POS[group[0]]
        rows = 2 * len(group)
        for k in kinds[s]:
            for dz in group:
                for w in range(2):
                    ci = (4 - k) * 8 + POS[dz]
                    stg[s, k][POS[dz] * 2 + w] = own[s][dz][tabs[k - 1, s, w * 32 + ci]]
        keep(own[s], s, 0, group)
        for k in kinds[s]:
            q = (4 - k) * 16 + 2 * p0
            crossed[s].append(
                go(
                    sems.copy(
                        stg[s, k].at[2 * p0 : 2 * p0 + rows], comp[s].at[q : q + rows], side[k]
                    )
                )
            )

    sent = {}

    def spatial(s):
        for c in crossed[s] + narrowed.get(s, []):
            c.wait_recv()
        far = [(t // 2 + k) % 4 for k in (2, 1, 3, 0)]
        sent[s] = []
        for part in ((0, 1), (2, 3)):
            summed = []
            for i in part:
                r = far[i]
                left = jnp.concatenate([tv[s, r, k] for k in range(8)], axis=1)
                right = jnp.concatenate([comp[s][slots[s, r, k]] for k in range(8)], axis=0)
                summed.append(dot(left, right).astype(jnp.bfloat16))
            for i, rows in zip(part, summed):
                hidden = jnp.maximum(dot(rows, weight[...]), 0.0).astype(jnp.bfloat16)
                hid[s, pl.ds(2 * far[i], 2)] = hidden.reshape(2, 64, 128)
            for i in part:
                for core in range(2):
                    if i < 3 or core:
                        peer = far[i] * 2 + (t + core) % 2
                        sent[s].append(
                            go(sems.copy(hid.at[s, peer], arr.at[t * 4 + s], dict(tm=peer)))
                        )
        arr[t * 4 + s] = hid[s, t]

    for s in ORDER:
        share(s, GROUPS[0])
    paired = {}

    def begin(s):
        swapped[s].wait_recv()
        paired[s] = ring(pair[s], 1)

    def advance(s, step):
        for c in paired[s]:
            c.wait_recv()
        if step == 1:
            paired[s] = ring(pair[s], 2)
            keep(pair[s], s, 2, GROUPS[0])
        else:
            narrow(s)
        keep(pair[s], s, 2, GROUPS[step])

    for s in EARLY:
        begin(s)
    for step in range(1, 5):
        for s in ORDER:
            for c in ringed[s]:
                c.wait_recv()
            if step < 4:
                ringed[s] = ring(own[s], step + 1)
            share(s, GROUPS[step])
        for s in EARLY:
            if step < 3:
                advance(s, step)
        if step == 1:
            hear(along, range(3, 7))
        if step == 3:
            for s in LATE:
                begin(s)
    for step in range(1, 3):
        for s in LATE:
            advance(s, step)
    loads[-1].wait()
    for s in DIRECT + EARLY:
        spatial(s)
    for s in LATE:
        spatial(s)
    for s in DIRECT + EARLY + LATE[:-1]:
        for c in sent[s]:
            c.wait_recv()

    @pl.loop(0, 4)
    def _(i):
        s = (3 + i) % 4

        @pl.when(i == 3)
        def _():
            for c in sent[2]:
                c.wait_recv()

        for k in range(4):
            project(8 * k + s, 8 * k + 4 + s, arr, pos, wcat, mix, proj)

    def block(j):
        g = j // 2
        return (t // 2 + 2 + g + g // 2 + 2 * (g // 3)) % 4 * 2 + (t + j + g // 3) % 2

    def back(j):
        return pltpu.make_async_remote_copy(
            obuf.at[j], oarr.at[:, t], send.at[sems.n + j], recv.at[sems.n + j],
            device_id=dict(tm=block(j)), device_id_type=MESH,
        )

    @pl.loop(0, 3)
    def _(g):
        blocks = [block(2 * g + i) for i in range(2)]
        for i, tb in enumerate(blocks):
            attend(tb, proj, att, 4 * i)
        obuf[pl.ds(2 * g, 2)] = finish(blocks, att, mix, wout, gain, mlp_up, mlp_down)
        for i in range(2):
            back(2 * g + i).start()

    @pl.loop(6, 8)
    def _(j):
        attend(block(j), proj, att)
        obuf[pl.ds(j, 1)] = finish([block(j)], att, mix, wout, gain, mlp_up, mlp_down)

        @pl.when(j == 6)
        def _():
            back(6).start()

    oarr[:, t] = obuf[7]

    for c in started:
        c.wait_send()

    @pl.loop(0, 7)
    def _(j):
        back(j).wait_recv()

    out[...] = oarr[...]

    @pl.loop(0, 7)
    def _(j):
        back(j).wait_send()

    assert sems.n + 7 == COPIES


def local(
    features, tile_cols, tile_vals, space_weight, positions, attn_proj, attn_out, norm_gain,
    mlp_up, mlp_down,
):
    half, word, single = jnp.bfloat16, jnp.int32, jnp.float32
    block4 = pltpu.VMEM((4, 128, 128), half)
    embedded = pl.pallas_call(
        kernel,
        out_shape=jax.ShapeDtypeStruct((4, 8, 64, 128), half),
        in_specs=[pl.BlockSpec(memory_space=pltpu.HBM)] * 10,
        out_specs=pl.BlockSpec(memory_space=pltpu.VMEM),
        scratch_shapes=[
            pltpu.VMEM((4, 4, 128, 128), half),
            pltpu.VMEM((4, 4, 8), word),
            pltpu.VMEM((4, 4, 8, 128, 128), half),
            pltpu.VMEM((128, 128), half),
            pltpu.VMEM((32, 128), half),
            pltpu.VMEM((128, 384), half),
            pltpu.VMEM((128, 128), half),
            pltpu.VMEM((1, 128), single),
            pltpu.VMEM((128, 512), half),
            pltpu.VMEM((512, 128), half),
            pltpu.VMEM((8, 128), word),
            pltpu.VMEM((4, 8, 128), word),
            pltpu.SMEM((8, 128), word),
            pltpu.SMEM((4, 8, 128), word),
            pltpu.VMEM((len(TABLE), 8, 128), word),
            pltpu.SMEM((len(TABLE), 8, 128), word),
            pltpu.VMEM((len(PAIRED), 2, 3, 128, 128), half),
            pltpu.VMEM((2 * 4 + len(DIRECT), 16, 128, 128), half),
            pltpu.VMEM((4, 8, 64, 128), half),
            pltpu.VMEM((32, 64, 128), half),
            pltpu.VMEM((192, 256), half),
            pltpu.VMEM((64, 256), half),
            pltpu.VMEM((32, 1, 128), single),
            pltpu.VMEM((32, 64, 128), half),
            pltpu.VMEM((32, 192, 128), single),
            pltpu.VMEM((16, 64, 128), single),
            pltpu.VMEM((8, 4, 64, 128), half),
            pltpu.VMEM((4, 8, 64, 128), half),
            pltpu.SemaphoreType.DMA((COPIES,)),
            pltpu.SemaphoreType.DMA((COPIES,)),
            pltpu.SemaphoreType.DMA((10,)),
        ]
        + [pltpu.VMEM((64, 128, 128), half)] * 4
        + [block4] * 28
        + [block4] * (5 * len(PAIRED)),
        compiler_params=pltpu.CompilerParams(
            collective_id=0, has_side_effects=True, vmem_limit_bytes=44 * 2**20
        ),
    )(
        *[
            pltpu.with_memory_space_constraint(a, pltpu.HBM)
            for a in (
                features.reshape(4, 4, 128, 128), tile_cols, tile_vals, space_weight, positions,
                attn_proj, attn_out, norm_gain.reshape(1, 128), mlp_up, mlp_down,
            )
        ]
    )
    return embedded.reshape(4, 512, 128)


def solution(mesh):
    placed = (
        P("tm", "vert", None),
        P("tm", "vert", None),
        P("tm", "vert", None, None, None),
        P(),
        P(),
        P(),
        P(),
        P(),
        P(),
        P(),
    )
    return jax.shard_map(
        local, mesh=mesh, in_specs=placed, out_specs=P("tm", "vert", None), check_vma=False
    )
```

```python
import math

import jax
import jax.numpy as jnp
from jax import lax
from jax.experimental import pallas as pl
from jax.experimental.pallas import tpu as pltpu
from jax.sharding import PartitionSpec as P

MESH = pl.DeviceIdType.MESH
norm_eps = 1e-05
SCORE = 1.0 / (4.0 * math.sqrt(8.0))
POWER = 4.0 * math.log2(math.e)

ZORD = (0, 1, 7, 2, 6, 3, 5, 4)
POS = {dz: p for p, dz in enumerate(ZORD)}
GROUPS = ((0,), (1, 7), (2, 6), (3, 5), (4,))
PAIRED = (0, 1, 2)
DIRECT = (3,)
EARLY, LATE = (0,), (1, 2)
ORDER = (3, 0, 1, 2)
TABLE = {(0, 1): 0, (0, 2): 1, (0, 3): 2, (1, 0): 3, (2, 0): 4, (7, 0): 5, (6, 0): 6}


def dot_t(a, b):
    return lax.dot_general(a, b, (((1,), (1,)), ((), ())), preferred_element_type=jnp.float32)


def dot(a, b):
    return jnp.dot(a, b, preferred_element_type=jnp.float32)


def arrange(attn_proj, attn_out, wcat, wout):
    row = lax.broadcasted_iota(jnp.int32, (192, 384), 0)
    col = lax.broadcasted_iota(jnp.int32, (192, 384), 1)
    base = (row // 64) * 128 + (row % 8) * 8 + (row // 8) % 8
    for half in range(2):
        pick = (col == base + half * 64).astype(jnp.bfloat16)
        wcat[:, half * 128 : (half + 1) * 128] = dot_t(pick, attn_proj[...]).astype(jnp.bfloat16)
    row = lax.broadcasted_iota(jnp.int32, (64, 128), 0)
    col = lax.broadcasted_iota(jnp.int32, (64, 128), 1)
    base = (row % 8) * 8 + row // 8
    for half in range(2):
        pick = (col == base + half * 64).astype(jnp.bfloat16)
        wout[:, half * 128 : (half + 1) * 128] = dot(pick, attn_out[...]).astype(jnp.bfloat16)


def project(t0, t1, arr, pos, wcat, mix, proj):
    zero = jnp.zeros((64, 128), jnp.bfloat16)
    rows = []
    for t in (t0, t1):
        m = (arr[t].astype(jnp.float32) + pos[t]).astype(jnp.bfloat16)
        mix[t] = m
        rows.append(jnp.concatenate([m, zero], axis=1))
        rows.append(jnp.concatenate([zero, m], axis=1))
    both = jnp.concatenate(rows, axis=0)
    p = dot_t(wcat[...], both).astype(jnp.bfloat16).astype(jnp.float32)
    for i, t in enumerate((t0, t1)):
        q = p[:, i * 128 : (i + 1) * 128]
        proj[t, 0:64] = q[0:64] * SCORE
        proj[t, 64:192] = q[64:192]


def attend(tb, proj, att, slot=0):
    def parts(t, k):
        return proj[t, 64 * k : 64 * (k + 1)].reshape(8, 8, 128)

    for pair in range(2):
        qs = [parts(4 * tb + 2 * pair + i, 0) for i in range(2)]

        def quad(uq, carry, diag):
            carry = list(carry)
            for ui in range(4):
                if diag and ui > 2 * pair + 1:
                    continue
                u = 4 * uq + ui
                k, v = parts(u, 1), parts(u, 2)
                for i in range(2):
                    if diag and ui > 2 * pair + i:
                        continue
                    e = jnp.exp2(POWER * jnp.tanh(jnp.sum(qs[i] * k, axis=0)))
                    carry[2 * i] = carry[2 * i] + e[None] * v
                    carry[2 * i + 1] = carry[2 * i + 1] + e
            return tuple(carry)

        zero = (jnp.zeros((8, 8, 128), jnp.float32), jnp.zeros((8, 128), jnp.float32)) * 2
        carry = lax.fori_loop(0, tb, lambda uq, c: quad(uq, c, False), zero)
        carry = quad(tb, carry, True)
        for i in range(2):
            a = carry[2 * i] * (1.0 / carry[2 * i + 1])[None]
            att[slot + 2 * pair + i] = a.reshape(64, 128)


def finish(blocks, att, mix, wout, gain, mlp_up, mlp_down):
    n = 4 * len(blocks)
    out = []
    for i in range(n):
        o = lax.dot_general(
            att[i].astype(jnp.bfloat16), wout[...], (((0,), (0,)), ((), ())),
            preferred_element_type=jnp.float32,
        )
        out.append(o[0:64, 0:128] + o[64:128, 128:256])
    out = jnp.concatenate(out, axis=0)
    m = jnp.concatenate([mix[pl.ds(4 * tb, 4)].reshape(256, 128) for tb in blocks], axis=0)
    stream = m.astype(jnp.float32) + out
    centre = jnp.mean(stream, axis=-1, keepdims=True)
    shifted = stream - centre
    spread = jnp.mean(shifted * shifted, axis=-1, keepdims=True)
    normed = (shifted * lax.rsqrt(spread + norm_eps) * gain[...]).astype(jnp.bfloat16)
    expanded = jnp.maximum(dot(normed, mlp_up[...]), 0.0).astype(jnp.bfloat16)
    done = (stream + dot(expanded, mlp_down[...])).astype(jnp.bfloat16)
    return done.reshape(len(blocks), 4, 64, 128)


def index_tables(z, x, cols, tab_v, slots_v):
    c = cols[...]
    lane = lax.broadcasted_iota(jnp.int32, (4, 4, 128), 2)
    tab = jnp.where(lane < 32, 3, 0)
    seen = []
    for k in range(8):
        ck = jnp.broadcast_to(c[:, :, k : k + 1], (4, 4, 128))
        blk = ck & 3
        dz = ((ck >> 4) - z) & 7
        dx = ((ck >> 2) - x) & 3
        pos = jnp.where(dz == 0, 0, jnp.where(dz <= 4, 2 * dz - 1, 16 - 2 * dz))
        ci = dx * 8 + pos
        seen.append((blk, ci))
        tab = jnp.where(
            ci == lane,
            jnp.minimum(tab, blk),
            jnp.where(ci + 32 == lane, jnp.maximum(tab, blk), tab),
        )
    low = jnp.min(tab, axis=1, keepdims=True)
    high = jnp.max(tab, axis=1, keepdims=True)
    tab = jnp.where(lane[:, 0:1] < 32, low, high)
    tab_v[...] = jnp.zeros((8, 128), jnp.int32)
    for s in range(4):
        tab_v[s : s + 1] = tab[s]
    slots = jnp.zeros((4, 4, 128), jnp.int32)
    for k, (blk, ci) in enumerate(seen):
        mine = jnp.sum(
            jnp.where(ci == lane, tab.astype(jnp.float32), 0.0), axis=2, keepdims=True
        )
        other = (blk.astype(jnp.float32) != mine).astype(jnp.int32)
        slots = jnp.where(lane == k, 2 * ci + other, slots)
    slots_v[...] = jnp.zeros((4, 8, 128), jnp.int32)
    slots_v[:, 0:4] = slots


class Sems:
    def __init__(self, send, recv):
        self.send, self.recv, self.n = send, recv, 0

    def copy(self, src, dst, device):
        i = self.n
        self.n += 1
        return pltpu.make_async_remote_copy(
            src, dst, self.send.at[i], self.recv.at[i], device_id=device, device_id_type=MESH
        )


COPIES = len(TABLE) + 4 * 8 + len(PAIRED) * (1 + 4 + 4) + 5 * (4 * 2 + len(DIRECT)) + 4 * 7 + 7


def kernel(
    feat_h, cols_h, tv_h, weight_h, positions_h, attn_proj_h, attn_out_h, gain_h, mlp_up_h,
    mlp_down_h, out,
    feat, cols, tv, weight, positions, attn_proj, attn_out, gain, mlp_up, mlp_down,
    tab_v, slots_v, tab_s, slots, tabr, tabs, picked, stg_refs, hid, arr, wcat, wout, pos, mix, proj, att,
    obuf, oarr, send, recv, lsem, *bufs,
):
    bufs = list(bufs)
    comp = [bufs.pop(0) for _ in range(4)]
    own = [{dz: bufs.pop(0) for dz in range(1, 8)} for _ in range(4)]
    pair = {s: {dz: bufs.pop(0) for dz in (0, 1, 2, 6, 7)} for s in PAIRED}
    for s in range(4):
        own[s][0] = feat.at[s]
    kinds = {s: (1, 3) if s in PAIRED else (1, 3, 2) for s in range(4)}
    stg = {}
    for s in range(4):
        for k in kinds[s]:
            stg[s, k] = stg_refs.at[len(stg)]

    v = lax.axis_index("vert")
    t = lax.axis_index("tm")
    z, x = v // 4, v % 4
    near = {r: dict(vert=((z + r[0]) % 8) * 4 + (x + r[1]) % 4) for r in TABLE}
    up, down = near[1, 0], near[7, 0]
    side = {k: near[0, k] for k in (1, 2, 3)}
    times = {k: dict(tm=(t + k) % 8) for k in range(1, 8)}

    barrier = pltpu.get_barrier_semaphore()
    peers = list(near.values()) + list(times.values())
    for peer in peers:
        pl.semaphore_signal(barrier, inc=1, device_id=peer, device_id_type=MESH)

    loads = [
        pltpu.make_async_copy(src, dst, lsem.at[i])
        for i, (src, dst) in enumerate(
            [
                (cols_h, cols), (feat_h, feat), (attn_proj_h, attn_proj), (attn_out_h, attn_out),
                (positions_h, positions), (weight_h, weight), (gain_h, gain), (mlp_up_h, mlp_up),
                (mlp_down_h, mlp_down), (tv_h, tv),
            ]
        )
    ]
    for c in loads[:-1]:
        c.start()
    loads[1].wait()
    pl.semaphore_wait(barrier, len(peers))

    sems = Sems(send, recv)
    started = []

    def go(copy):
        copy.start()
        started.append(copy)
        return copy

    def ring(buf, step):
        if step < 4:
            a = sems.copy(buf[(9 - step) % 8], buf[8 - step], up)
            b = sems.copy(buf[step - 1], buf[step], down)
        else:
            a = sems.copy(buf[5].at[0:2], buf[4].at[0:2], up)
            b = sems.copy(buf[3].at[2:4], buf[4].at[2:4], down)
        return go(a), go(b)

    def place(dx, dz):
        return 2 * (dx * 8 + POS[dz])

    def narrow(s):
        ends = ((6, (1, 0), (2, 0), 5), (2, (7, 0), (6, 0), 3))
        for way, (dz, first, second, end) in enumerate(ends):
            part = picked.at[PAIRED.index(s), way]
            part[2] = pair[s][dz][tabs[TABLE[second], s, 32 * way + 16 + POS[4]]]
            for w in range(2):
                part[w] = pair[s][dz][tabs[TABLE[first], s, 32 * w + 16 + POS[end]]]
        for way, (dz, first, second, end) in enumerate(ends):
            part = picked.at[PAIRED.index(s), way]
            q = place(2, 4) + way
            narrowed[s].append(
                go(sems.copy(part.at[2:3], comp[s].at[q : q + 1], near[second]))
            )
            q = place(2, end)
            narrowed[s].append(go(sems.copy(part.at[0:2], comp[s].at[q : q + 2], near[first])))

    narrowed = {s: [] for s in PAIRED}
    ringed = {ORDER[0]: ring(own[ORDER[0]], 1)}

    def swap(s):
        return go(sems.copy(feat.at[s], pair[s][0], side[2]))

    swapped = {PAIRED[0]: swap(PAIRED[0])}
    loads[0].wait()
    index_tables(z, x, cols, tab_v, slots_v)

    def tell(r):
        return go(sems.copy(tab_v, tabr.at[TABLE[(8 - r[0]) % 8, (4 - r[1]) % 4]], near[r]))

    def hear(tables, held):
        for c in tables:
            c.wait_recv()
        held = [pltpu.make_async_copy(tabr.at[k], tabs.at[k], lsem.at[2 + k]) for k in held]
        for c in held:
            c.start()
        for c in held:
            c.wait()

    sideways = [tell(r) for r in TABLE if r[1]]
    swapped |= {s: swap(s) for s in PAIRED[1:]}
    for s in ORDER[1:]:
        ringed[s] = ring(own[s], 1)
    along = [tell(r) for r in TABLE if r[0]]
    mine = [
        pltpu.make_async_copy(tab_v, tab_s, lsem.at[0]),
        pltpu.make_async_copy(slots_v, slots, lsem.at[1]),
    ]
    for c in loads[2:-1]:
        c.wait()
    for c in mine:
        c.start()
    arrange(attn_proj, attn_out, wcat, wout)
    pos[...] = positions[...].astype(jnp.float32).reshape(32, 1, 128)
    for c in mine:
        c.wait()
    hear(sideways, range(3))
    loads[-1].start()
    crossed = {s: [] for s in range(4)}

    def keep(buf, s, dx, group):
        for dz in group:
            ci = dx * 8 + POS[dz]
            for w in range(2):
                comp[s][ci * 2 + w] = buf[dz][tab_s[s, w * 32 + ci]]

    def share(s, group):
        p0 = POS[group[0]]
        rows = 2 * len(group)
        for k in kinds[s]:
            for dz in group:
                for w in range(2):
                    ci = (4 - k) * 8 + POS[dz]
                    stg[s, k][POS[dz] * 2 + w] = own[s][dz][tabs[k - 1, s, w * 32 + ci]]
        keep(own[s], s, 0, group)
        for k in kinds[s]:
            q = (4 - k) * 16 + 2 * p0
            crossed[s].append(
                go(
                    sems.copy(
                        stg[s, k].at[2 * p0 : 2 * p0 + rows], comp[s].at[q : q + rows], side[k]
                    )
                )
            )

    sent = {}

    def spatial(s):
        for c in crossed[s] + narrowed.get(s, []):
            c.wait_recv()
        far = [(t // 2 + k) % 4 for k in (2, 1, 3, 0)]
        sent[s] = []
        for part in ((0, 1), (2, 3)):
            summed = []
            for i in part:
                r = far[i]
                left = jnp.concatenate([tv[s, r, k] for k in range(8)], axis=1)
                right = jnp.concatenate([comp[s][slots[s, r, k]] for k in range(8)], axis=0)
                summed.append(dot(left, right).astype(jnp.bfloat16))
            for i, rows in zip(part, summed):
                hidden = jnp.maximum(dot(rows, weight[...]), 0.0).astype(jnp.bfloat16)
                hid[s, pl.ds(2 * far[i], 2)] = hidden.reshape(2, 64, 128)
            for i in part:
                for core in range(2):
                    if i < 3 or core:
                        peer = far[i] * 2 + (t + core) % 2
                        sent[s].append(
                            go(sems.copy(hid.at[s, peer], arr.at[t * 4 + s], dict(tm=peer)))
                        )
        arr[t * 4 + s] = hid[s, t]

    for s in ORDER:
        share(s, GROUPS[0])
    paired = {}

    def begin(s):
        swapped[s].wait_recv()
        paired[s] = ring(pair[s], 1)

    def advance(s, step):
        for c in paired[s]:
            c.wait_recv()
        if step == 1:
            paired[s] = ring(pair[s], 2)
            keep(pair[s], s, 2, GROUPS[0])
        else:
            narrow(s)
        keep(pair[s], s, 2, GROUPS[step])

    for s in EARLY:
        begin(s)
    for step in range(1, 5):
        for s in ORDER:
            for c in ringed[s]:
                c.wait_recv()
            if step < 4:
                ringed[s] = ring(own[s], step + 1)
            share(s, GROUPS[step])
        for s in EARLY:
            if step < 3:
                advance(s, step)
        if step == 1:
            hear(along, range(3, 7))
        if step in (2, 3):
            begin(LATE[step - 2])
    for step in range(1, 3):
        for s in LATE:
            advance(s, step)
    loads[-1].wait()
    for s in DIRECT + EARLY:
        spatial(s)
    for s in LATE:
        spatial(s)
    for s in DIRECT + EARLY + LATE[:-1]:
        for c in sent[s]:
            c.wait_recv()

    @pl.loop(0, 4)
    def _(i):
        s = (3 + i) % 4

        @pl.when(i == 3)
        def _():
            for c in sent[2]:
                c.wait_recv()

        for k in range(4):
            project(8 * k + s, 8 * k + 4 + s, arr, pos, wcat, mix, proj)

    def block(j):
        g = j // 2
        return (t // 2 + 2 + g + g // 2 + 2 * (g // 3)) % 4 * 2 + (t + j + g // 3) % 2

    def back(j):
        return pltpu.make_async_remote_copy(
            obuf.at[j], oarr.at[:, t], send.at[sems.n + j], recv.at[sems.n + j],
            device_id=dict(tm=block(j)), device_id_type=MESH,
        )

    @pl.loop(0, 3)
    def _(g):
        blocks = [block(2 * g + i) for i in range(2)]
        for i, tb in enumerate(blocks):
            attend(tb, proj, att, 4 * i)
        obuf[pl.ds(2 * g, 2)] = finish(blocks, att, mix, wout, gain, mlp_up, mlp_down)
        for i in range(2):
            back(2 * g + i).start()

    @pl.loop(6, 8)
    def _(j):
        attend(block(j), proj, att)
        obuf[pl.ds(j, 1)] = finish([block(j)], att, mix, wout, gain, mlp_up, mlp_down)

        @pl.when(j == 6)
        def _():
            back(6).start()

    oarr[:, t] = obuf[7]

    for c in started:
        c.wait_send()

    @pl.loop(0, 7)
    def _(j):
        back(j).wait_recv()

    out[...] = oarr[...]

    @pl.loop(0, 7)
    def _(j):
        back(j).wait_send()

    assert sems.n + 7 == COPIES


def local(
    features, tile_cols, tile_vals, space_weight, positions, attn_proj, attn_out, norm_gain,
    mlp_up, mlp_down,
):
    half, word, single = jnp.bfloat16, jnp.int32, jnp.float32
    block4 = pltpu.VMEM((4, 128, 128), half)
    embedded = pl.pallas_call(
        kernel,
        out_shape=jax.ShapeDtypeStruct((4, 8, 64, 128), half),
        in_specs=[pl.BlockSpec(memory_space=pltpu.HBM)] * 10,
        out_specs=pl.BlockSpec(memory_space=pltpu.VMEM),
        scratch_shapes=[
            pltpu.VMEM((4, 4, 128, 128), half),
            pltpu.VMEM((4, 4, 8), word),
            pltpu.VMEM((4, 4, 8, 128, 128), half),
            pltpu.VMEM((128, 128), half),
            pltpu.VMEM((32, 128), half),
            pltpu.VMEM((128, 384), half),
            pltpu.VMEM((128, 128), half),
            pltpu.VMEM((1, 128), single),
            pltpu.VMEM((128, 512), half),
            pltpu.VMEM((512, 128), half),
            pltpu.VMEM((8, 128), word),
            pltpu.VMEM((4, 8, 128), word),
            pltpu.SMEM((8, 128), word),
            pltpu.SMEM((4, 8, 128), word),
            pltpu.VMEM((len(TABLE), 8, 128), word),
            pltpu.SMEM((len(TABLE), 8, 128), word),
            pltpu.VMEM((len(PAIRED), 2, 3, 128, 128), half),
            pltpu.VMEM((2 * 4 + len(DIRECT), 16, 128, 128), half),
            pltpu.VMEM((4, 8, 64, 128), half),
            pltpu.VMEM((32, 64, 128), half),
            pltpu.VMEM((192, 256), half),
            pltpu.VMEM((64, 256), half),
            pltpu.VMEM((32, 1, 128), single),
            pltpu.VMEM((32, 64, 128), half),
            pltpu.VMEM((32, 192, 128), single),
            pltpu.VMEM((16, 64, 128), single),
            pltpu.VMEM((8, 4, 64, 128), half),
            pltpu.VMEM((4, 8, 64, 128), half),
            pltpu.SemaphoreType.DMA((COPIES,)),
            pltpu.SemaphoreType.DMA((COPIES,)),
            pltpu.SemaphoreType.DMA((10,)),
        ]
        + [pltpu.VMEM((64, 128, 128), half)] * 4
        + [block4] * 28
        + [block4] * (5 * len(PAIRED)),
        compiler_params=pltpu.CompilerParams(
            collective_id=0, has_side_effects=True, vmem_limit_bytes=44 * 2**20
        ),
    )(
        *[
            pltpu.with_memory_space_constraint(a, pltpu.HBM)
            for a in (
                features.reshape(4, 4, 128, 128), tile_cols, tile_vals, space_weight, positions,
                attn_proj, attn_out, norm_gain.reshape(1, 128), mlp_up, mlp_down,
            )
        ]
    )
    return embedded.reshape(4, 512, 128)


def solution(mesh):
    placed = (
        P("tm", "vert", None),
        P("tm", "vert", None),
        P("tm", "vert", None, None, None),
        P(),
        P(),
        P(),
        P(),
        P(),
        P(),
        P(),
    )
    return jax.shard_map(
        local, mesh=mesh, in_specs=placed, out_specs=P("tm", "vert", None), check_vma=False
    )
```
